32 devices in a mesh: fsdp: 8 (over z, y), tp: 4 (over x, core).
Axes of the slice: x: 2, y: 2, z: 4, core: 2. Of those that a mesh axis runs over, the one named last changes fastest.
Arguments:
- layer_input: bfloat16 [8192, 768], P(('fsdp', 'tp')), may hold values from -12 to 12
- out_cotangent: bfloat16 [8192, 768], P(('fsdp', 'tp')), may hold values from -12 to 12
- segments: int32 [8, 1024], P('fsdp'), may hold values from 0 to 3, never falling along the last dimension, each value on 1 to 512 neighbouring positions
- norm_gain: float32 [768], replicated, may hold values from 0.5 to 1.5
- norm_bias: float32 [768], replicated, may hold values from -3 to 3
- qkv_weight: bfloat16 [768, 2304], P('fsdp', 'tp'), may hold values from -20 to 20
- qkv_bias: float32 [2304], P('tp'), may hold values from -3 to 3
- out_weight: bfloat16 [768, 768], P('tp', 'fsdp'), may hold values from -0.875 to 0.875
- out_bias: float32 [768], replicated, may hold values from -3 to 3
- up_weight: bfloat16 [768, 3072], P('fsdp', 'tp'), may hold values from -0.21875 to 0.21875
- up_bias: float32 [3072], P('tp'), may hold values from -3 to 3
- down_weight: bfloat16 [3072, 768], P('tp', 'fsdp'), may hold values from -0.109375 to 0.109375
- down_bias: float32 [768], replicated, may hold values from -3 to 3
Outputs:
- layer_output: bfloat16 [8192, 768], P(('fsdp', 'tp'))
- input_grad: bfloat16 [8192, 768], P(('fsdp', 'tp'))
- norm_gain_grad: float32 [768], replicated
- norm_bias_grad: float32 [768], replicated
- qkv_weight_grad: float32 [768, 2304], P('fsdp', 'tp')
- qkv_bias_grad: float32 [2304], P('tp')
- out_weight_grad: float32 [768, 768], P('tp', 'fsdp')
- out_bias_grad: float32 [768], replicated
- up_weight_grad: float32 [768, 3072], P('fsdp', 'tp')
- up_bias_grad: float32 [3072], P('tp')
- down_weight_grad: float32 [3072, 768], P('tp', 'fsdp')
- down_bias_grad: float32 [768], replicated
The draws below stay inside these ranges and needn't reach their ends.
Inputs may be any that keep to these rules, and one draw needn't show every extreme that they name: `segments`: each row is one sequence of 1024 tokens; its numbers name documents, never fall along the row, and each document spans 1 to 512 tokens, one exactly 512.
All inputs are finite; a program needn't handle non-finite values.
Results may differ from the reference program's by a relative error of at most 0.01.
Values may be sent and summed in bfloat16 or wider, within the bound.
A program may use at most 128 MiB of HBM per device.

```python
import math
import jax
import jax.numpy as jnp
import numpy as np
from jax import lax

D = 768
HEADS = 12
HEAD_DIM = 64
FF = 3072
ROT = 16
SEQ = 1024
SEQS = 8
TOKENS = 8192
DOCS = 4
MOST = 512


def draw_qkv_weight(key, part):
    drawn = jnp.clip(jax.random.normal(key, (D, HEADS, 3, HEAD_DIM), jnp.float32), -6.0, 6.0) * D ** (-0.5)
    return drawn.reshape(D, 3 * D).astype(jnp.bfloat16)


def strengthened(array, rng, source, target, blocks, factor):
    owner, partner = [(jnp.arange(array.shape[position]) // (array.shape[position] // blocks)).reshape([-1 if axis == position else 1 for axis in range(array.ndim)]) for position in (source, target)]
    chosen = jax.random.permutation(rng, blocks)[partner]
    strong = (owner == chosen) | (owner == (partner + blocks // 2) % blocks)
    return jnp.where(strong, factor * array, array)


def steps_of(rng, extent, shards, least, high):
    level = 1.0
    for dim, blocks in shards:
        heights = jax.random.uniform(jax.random.fold_in(jax.random.fold_in(rng, 6), dim), (blocks,), jnp.float32, least / len(shards), high / len(shards))
        level = level * jnp.repeat(jnp.exp(heights), extent[dim] // blocks).reshape((-1,) + (1,) * (len(extent) - 1 - dim))
    return level


def profile(number_of, total, most, lean):
    portions = [(1 << 20) // math.isqrt(grade ** lean) + 1 for grade in range(2, number_of + 1)]
    rest, holding = total - most - (number_of - 1), [1] * (number_of - 1)
    while rest > 0:
        candidates = [i for i in range(number_of - 1) if holding[i] < most]
        mass, budget = sum([portions[i] for i in candidates]), rest
        for i in candidates:
            addition = min(most - holding[i], max(1, budget * portions[i] // mass), rest)
            holding[i] = holding[i] + addition
            rest = rest - addition
    return np.array([most] + holding)


def uneven_parts(stream_key, number_of, total, bound, skew):
    if number_of == 2:
        one = jax.random.randint(stream_key, (), max(1, total - bound), min(bound, total - 1) + 1)
        return jnp.stack([one, total - one])
    tallies = jnp.asarray(profile(number_of, total, bound, skew), jnp.int32)
    couples = (number_of - 1) // 2
    giver, taker = tallies[1:1 + 2 * couples:2], tallies[2:2 + 2 * couples:2]
    margin = jnp.minimum(giver - 1, bound - taker)
    passed = jax.random.randint(jax.random.fold_in(stream_key, 1), (couples,), 0, 1 << 20) % (margin + 1)
    tallies = tallies.at[1:1 + 2 * couples:2].set(giver - passed).at[2:2 + 2 * couples:2].set(taker + passed)
    return tallies[jax.random.permutation(jax.random.fold_in(stream_key, 2), number_of)]


def normal_values(key, shape, width, reach, cuts=(), held_as=jnp.bfloat16):
    entries = jax.random.normal(key, shape, jnp.float32) * width
    if len(cuts) > 0:
        entries = steps_of(key, shape, cuts, -0.22, 0.18) * entries
    return jnp.clip(entries, min=-reach, max=reach).astype(held_as)


def noise_with(key, dims, deviation, most, pieces, heavy, kind=jnp.bfloat16):
    values = deviation * jax.random.normal(key, dims, jnp.float32)
    if pieces:
        values = values * steps_of(key, dims, pieces, -0.22, 0.18)
    return jnp.clip(strengthened(values, jax.random.fold_in(key, 3), *heavy), -most, most).astype(kind)


def setup_inputs(seed: int = 0) -> dict:
    key_list = jax.random.split(jax.random.key(seed), 14)
    layer_input = noise_with(key_list[0], (TOKENS, D), 1.0, 12.0, ((0, 32),), (0, 1, 32, 2.75))
    out_cotangent = noise_with(key_list[1], (TOKENS, D), 1.0, 12.0, ((0, 32),), (0, 1, 32, 2.75))
    segments = jax.vmap(lambda own: jnp.searchsorted(jnp.cumsum(uneven_parts(own, DOCS, SEQ, MOST, 1)), jnp.arange(SEQ), side="right"))(jax.random.split(key_list[2], SEQS)).reshape((SEQS, SEQ)).astype(jnp.int32)
    norm_gain = jnp.clip(1.0 + 0.1 * jax.random.normal(key_list[3], (D,), jnp.float32), 0.5, 1.5)
    norm_bias = normal_values(key_list[4], (D,), 0.5, 3.0, (), jnp.float32)
    qkv_weight = draw_qkv_weight(jax.random.fold_in(key_list[13], 71), 0)
    qkv_bias = normal_values(key_list[6], (3 * D,), 0.5, 3.0, ((0, 4),), jnp.float32)
    out_weight = normal_values(key_list[7], (D, D), (D // 16) ** -0.5, 0.875, ((0, 4), (1, 8)))
    out_bias = normal_values(key_list[8], (D,), 0.5, 3.0, (), jnp.float32)
    up_weight = normal_values(key_list[9], (D, FF), D ** -0.5, 0.21875, ((0, 8), (1, 4)))
    up_bias = normal_values(key_list[10], (FF,), 0.5, 3.0, ((0, 4),), jnp.float32)
    down_weight = normal_values(key_list[11], (FF, D), FF ** -0.5, 0.109375, ((0, 4), (1, 8)))
    down_bias = normal_values(key_list[12], (D,), 0.5, 3.0, (), jnp.float32)
    return dict(layer_input=layer_input, out_cotangent=out_cotangent, segments=segments, norm_gain=norm_gain, norm_bias=norm_bias, qkv_weight=qkv_weight, qkv_bias=qkv_bias, out_weight=out_weight, out_bias=out_bias, up_weight=up_weight, up_bias=up_bias, down_weight=down_weight, down_bias=down_bias)


EPSILON = 1e-05
ROTARY_BASE = 10000.0

def layer_norm(values, gain, shift):
    center = values - lax.optimization_barrier(jnp.mean(values, axis=-1, keepdims=True))
    spread = lax.optimization_barrier(jnp.mean(center * center, axis=-1, keepdims=True))
    inverse = lax.rsqrt(spread + EPSILON)
    normed = center * inverse
    return (normed, inverse, normed * gain + shift)

def gelu_value(pre_act):
    return 0.5 * pre_act * (1.0 + lax.erf(pre_act * 0.7071067811865476))

def gelu_slope(pre_act):
    return 0.5 * (1.0 + lax.erf(pre_act * 0.7071067811865476)) + pre_act * jnp.exp(-0.5 * pre_act * pre_act) * 0.3989422804014327

def positions_of(segment_row):
    length = segment_row.shape[0]
    counter = jnp.arange(length, dtype=jnp.int32)
    is_start = jnp.concatenate([jnp.ones((1,), dtype=jnp.bool_), segment_row[1:] != segment_row[:-1]])
    starts = lax.cummax(jnp.where(is_start, counter, jnp.zeros_like(counter)), axis=0)
    return counter - starts

def rotary_tables(positions):
    halves = ROT // 2
    inverse_freq = ROTARY_BASE ** (-(jnp.arange(halves, dtype=jnp.float32) * 2.0) / ROT)
    angles = positions.astype(jnp.float32)[:, None] * inverse_freq[None, :]
    cos_table = jnp.cos(angles)
    sin_table = jnp.sin(angles)
    return (jnp.concatenate([cos_table, cos_table], axis=-1), jnp.concatenate([sin_table, sin_table], axis=-1))

def rotate(tensor, cos_table, sin_table):
    halves = ROT // 2
    turned_part = tensor[..., :ROT]
    turned = jnp.concatenate([-turned_part[..., halves:], turned_part[..., :halves]], axis=-1)
    spun = turned_part * cos_table[:, None, :] + turned * sin_table[:, None, :]
    return jnp.concatenate([spun, tensor[..., ROT:]], axis=-1)

def unrotate(grad_in, cos_table, sin_table):
    halves = ROT // 2
    turned_part = grad_in[..., :ROT]
    scaled = turned_part * sin_table[:, None, :]
    back = jnp.concatenate([scaled[..., halves:], -scaled[..., :halves]], axis=-1)
    return jnp.concatenate([turned_part * cos_table[:, None, :] + back, grad_in[..., ROT:]], axis=-1)

def scores_of(queries, keys_in, allowed, score_scale):
    scores = jnp.einsum('qhd,khd->hqk', queries.astype(jnp.float32), keys_in.astype(jnp.float32)) * score_scale
    return jnp.where(allowed[None], scores, -jnp.inf)

def attend(queries, keys_in, values_in, allowed, score_scale):
    scores = scores_of(queries, keys_in, allowed, score_scale)
    highest = lax.optimization_barrier(jnp.max(scores, axis=-1, keepdims=True))
    log_total = highest + jnp.log(lax.optimization_barrier(jnp.sum(jnp.exp(scores - highest), axis=-1, keepdims=True)))
    weights = jnp.exp(scores - log_total).astype(jnp.bfloat16)
    mixed = jnp.einsum('hqk,khd->qhd', weights.astype(jnp.float32), values_in.astype(jnp.float32))
    return (mixed.astype(jnp.bfloat16), log_total)

def attend_back(queries, keys_in, values_in, mixed, grad_mixed, log_total, allowed, score_scale):
    scores = scores_of(queries, keys_in, allowed, score_scale)
    probs = jnp.exp(scores - log_total)
    weights = probs.astype(jnp.bfloat16)
    delta = lax.optimization_barrier(jnp.sum(grad_mixed.astype(jnp.float32) * mixed.astype(jnp.float32), axis=-1))
    grad_values = jnp.einsum('hqk,qhd->khd', weights.astype(jnp.float32), grad_mixed.astype(jnp.float32))
    grad_probs = jnp.einsum('qhd,khd->hqk', grad_mixed.astype(jnp.float32), values_in.astype(jnp.float32))
    grad_scores = (probs * (grad_probs - delta.T[:, :, None]) * score_scale).astype(jnp.bfloat16)
    grad_queries = jnp.einsum('hqk,khd->qhd', grad_scores.astype(jnp.float32), keys_in.astype(jnp.float32))
    grad_keys = jnp.einsum('hqk,qhd->khd', grad_scores.astype(jnp.float32), queries.astype(jnp.float32))
    return (grad_queries, grad_keys, grad_values)

def reference(layer_input, out_cotangent, segments, norm_gain, norm_bias, qkv_weight, qkv_bias, out_weight, out_bias, up_weight, up_bias, down_weight, down_bias):
    score_scale = HEAD_DIM ** (-0.5)
    inputs_seq = layer_input.reshape(SEQS, SEQ, D)
    cotan_seq = out_cotangent.reshape(SEQS, SEQ, D)

    def one_sequence(carry, member):
        input_rows, cotan_rows, segment_row = member
        own_rows = input_rows.astype(jnp.float32)
        normed, inverse, shifted = layer_norm(own_rows, norm_gain, norm_bias)
        features = shifted.astype(jnp.bfloat16)
        packed = (jnp.dot(features, qkv_weight, preferred_element_type=jnp.float32) + qkv_bias).reshape(SEQ, HEADS, 3, HEAD_DIM)
        cos_table, sin_table = rotary_tables(positions_of(segment_row))
        queries = rotate(packed[:, :, 0], cos_table, sin_table).astype(jnp.bfloat16)
        keys_all = rotate(packed[:, :, 1], cos_table, sin_table).astype(jnp.bfloat16)
        values_all = packed[:, :, 2].astype(jnp.bfloat16)
        counter = jnp.arange(SEQ, dtype=jnp.int32)
        allowed = (segment_row[:, None] == segment_row[None, :]) & (counter[:, None] >= counter[None, :])
        mixed, log_total = attend(queries, keys_all, values_all, allowed, score_scale)
        mixed_rows = mixed.reshape(SEQ, D)
        pre_act = jnp.dot(features, up_weight, preferred_element_type=jnp.float32) + up_bias
        gelu_rows = gelu_value(pre_act).astype(jnp.bfloat16)
        branch = jnp.dot(mixed_rows, out_weight, preferred_element_type=jnp.float32) + jnp.dot(gelu_rows, down_weight, preferred_element_type=jnp.float32)
        output_rows = (own_rows + branch + out_bias + down_bias).astype(jnp.bfloat16)
        cot_rows = cotan_rows.astype(jnp.float32)
        down_grad = jnp.dot(gelu_rows.T, cotan_rows, preferred_element_type=jnp.float32)
        grad_pre = jnp.dot(cotan_rows, down_weight.T, preferred_element_type=jnp.float32) * gelu_slope(pre_act)
        pre_grads = grad_pre.astype(jnp.bfloat16)
        up_grad = jnp.dot(features.T, pre_grads, preferred_element_type=jnp.float32)
        up_bias_part = lax.optimization_barrier(jnp.sum(grad_pre, axis=0))
        feature_grad = jnp.dot(pre_grads, up_weight.T, preferred_element_type=jnp.float32)
        out_grad = jnp.dot(mixed_rows.T, cotan_rows, preferred_element_type=jnp.float32)
        mixed_grad = jnp.dot(cotan_rows, out_weight.T, preferred_element_type=jnp.float32).astype(jnp.bfloat16).reshape(SEQ, HEADS, HEAD_DIM)
        grad_q, grad_k, grad_v = attend_back(queries, keys_all, values_all, mixed, mixed_grad, log_total, allowed, score_scale)
        grad_q = unrotate(grad_q, cos_table, sin_table)
        grad_k = unrotate(grad_k, cos_table, sin_table)
        packed_grad = jnp.stack([grad_q, grad_k, grad_v], axis=2).reshape(SEQ, 3 * D)
        qkv_bias_part = lax.optimization_barrier(jnp.sum(packed_grad, axis=0))
        packed_bf = packed_grad.astype(jnp.bfloat16)
        qkv_grad = jnp.dot(features.T, packed_bf, preferred_element_type=jnp.float32)
        feature_grad = feature_grad + jnp.dot(packed_bf, qkv_weight.T, preferred_element_type=jnp.float32)
        gain_part = lax.optimization_barrier(jnp.sum(feature_grad * normed, axis=0))
        shift_part = lax.optimization_barrier(jnp.sum(feature_grad, axis=0))
        scaled = feature_grad * norm_gain
        input_rows_grad = cot_rows + inverse * (scaled - lax.optimization_barrier(jnp.mean(scaled, axis=-1, keepdims=True)) - normed * lax.optimization_barrier(jnp.mean(scaled * normed, axis=-1, keepdims=True)))
        bias_part = lax.optimization_barrier(jnp.sum(cot_rows, axis=0))
        parts = (gain_part, shift_part, qkv_grad, qkv_bias_part, out_grad, bias_part, up_grad, up_bias_part, down_grad)
        carry = tuple((total + piece for total, piece in zip(carry, parts)))
        return (carry, (output_rows, input_rows_grad.astype(jnp.bfloat16)))
    start_carry = (jnp.zeros((D,), jnp.float32), jnp.zeros((D,), jnp.float32), jnp.zeros((D, 3 * D), jnp.float32), jnp.zeros((3 * D,), jnp.float32), jnp.zeros((D, D), jnp.float32), jnp.zeros((D,), jnp.float32), jnp.zeros((D, FF), jnp.float32), jnp.zeros((FF,), jnp.float32), jnp.zeros((FF, D), jnp.float32))
    totals, stacked = lax.scan(one_sequence, start_carry, (inputs_seq, cotan_seq, segments))
    layer_output = stacked[0].reshape(TOKENS, D)
    input_grad = stacked[1].reshape(TOKENS, D)
    gain_grad, shift_grad, qkv_grad, qkv_bias_grad, out_grad, bias_grad, up_grad, up_bias_grad, down_grad = totals
    return (layer_output, input_grad, gain_grad, shift_grad, qkv_grad, qkv_bias_grad, out_grad, bias_grad, up_grad, up_bias_grad, down_grad, bias_grad)
```

```python
import functools

import jax
import jax.numpy as jnp
from jax import lax
from jax.experimental import pallas as pl
from jax.experimental.pallas import tpu as pltpu
from jax.sharding import PartitionSpec as P

HEAD_DIM = 64
ROT = 16


EPSILON = 1e-05
ROTARY_BASE = 10000.0


def layer_norm(values, gain, shift):
    center = values - jnp.mean(values, axis=-1, keepdims=True)
    spread = jnp.mean(center * center, axis=-1, keepdims=True)
    inverse = lax.rsqrt(spread + EPSILON)
    normed = center * inverse
    return (normed, inverse, normed * gain + shift)


def gelu_value(pre_act):
    return 0.5 * pre_act * (1.0 + lax.erf(pre_act * 0.7071067811865476))


def gelu_slope(pre_act):
    return (
        0.5 * (1.0 + lax.erf(pre_act * 0.7071067811865476))
        + pre_act * jnp.exp(-0.5 * pre_act * pre_act) * 0.3989422804014327
    )


def positions_of(segment_row):
    length = segment_row.shape[0]
    counter = jnp.arange(length, dtype=jnp.int32)
    is_start = jnp.concatenate(
        [jnp.ones((1,), dtype=jnp.bool_), segment_row[1:] != segment_row[:-1]]
    )
    starts = lax.cummax(jnp.where(is_start, counter, jnp.zeros_like(counter)), axis=0)
    return counter - starts


def rotary_tables(positions):
    halves = ROT // 2
    inverse_freq = ROTARY_BASE ** (-(jnp.arange(halves, dtype=jnp.float32) * 2.0) / ROT)
    angles = positions.astype(jnp.float32)[:, None] * inverse_freq[None, :]
    cos_table = jnp.cos(angles)
    sin_table = jnp.sin(angles)
    return (
        jnp.concatenate([cos_table, cos_table], axis=-1),
        jnp.concatenate([sin_table, sin_table], axis=-1),
    )


def rotate(tensor, cos_table, sin_table):
    halves = ROT // 2
    turned_part = tensor[..., :ROT]
    turned = jnp.concatenate([-turned_part[..., halves:], turned_part[..., :halves]], axis=-1)
    spun = turned_part * cos_table[:, None, :] + turned * sin_table[:, None, :]
    return jnp.concatenate([spun, tensor[..., ROT:]], axis=-1)


def unrotate(grad_in, cos_table, sin_table):
    halves = ROT // 2
    turned_part = grad_in[..., :ROT]
    scaled = turned_part * sin_table[:, None, :]
    back = jnp.concatenate([scaled[..., halves:], -scaled[..., :halves]], axis=-1)
    return jnp.concatenate(
        [turned_part * cos_table[:, None, :] + back, grad_in[..., ROT:]], axis=-1
    )


def cross_rows(left, right):
    return lax.dot_general(
        left, right, (((0,), (0,)), ((), ())), preferred_element_type=jnp.float32
    )


def cross_cols(left, right):
    return lax.dot_general(
        left, right, (((1,), (1,)), ((), ())), preferred_element_type=jnp.float32
    )


def block_scores(queries, keys_in, segment_row, first_row, last_row, score_scale):
    counter = jnp.arange(last_row, dtype=jnp.int32)
    allowed = (segment_row[first_row:last_row, None] == segment_row[None, :last_row]) & (
        counter[first_row:last_row, None] >= counter[None, :last_row]
    )
    scores = cross_cols(queries[first_row:last_row], keys_in[:last_row]) * score_scale
    return jnp.where(allowed, scores, -jnp.inf)


def head_forward(queries, keys_in, values_in, segment_row, score_scale):
    length = queries.shape[0]
    span = min(512, length)
    mixed_parts = []
    total_parts = []
    for first_row in range(0, length, span):
        last_row = min(first_row + span, length)
        scores = block_scores(queries, keys_in, segment_row, first_row, last_row, score_scale)
        highest = jnp.max(scores, axis=-1, keepdims=True)
        log_total = highest + jnp.log(jnp.sum(jnp.exp(scores - highest), axis=-1, keepdims=True))
        weights = jnp.exp(scores - log_total).astype(jnp.bfloat16)
        mixed_parts.append(
            jnp.dot(weights, values_in[:last_row], preferred_element_type=jnp.float32).astype(
                jnp.bfloat16
            )
        )
        total_parts.append(log_total)
    return (jnp.concatenate(mixed_parts, axis=0), jnp.concatenate(total_parts, axis=0))


def head_backward(
    queries, keys_in, values_in, mixed, grad_mixed, log_total, segment_row, score_scale
):
    length = queries.shape[0]
    span = min(512, length)
    delta = jnp.sum(
        grad_mixed.astype(jnp.float32) * mixed.astype(jnp.float32), axis=-1, keepdims=True
    )
    grad_keys = jnp.zeros(keys_in.shape, jnp.float32)
    grad_values = jnp.zeros(values_in.shape, jnp.float32)
    query_parts = []
    for first_row in range(0, length, span):
        last_row = min(first_row + span, length)
        padding = ((0, length - last_row), (0, 0))
        scores = block_scores(queries, keys_in, segment_row, first_row, last_row, score_scale)
        probs = jnp.exp(scores - log_total[first_row:last_row])
        weights = probs.astype(jnp.bfloat16)
        grad_rows = grad_mixed[first_row:last_row]
        grad_values = grad_values + jnp.pad(cross_rows(weights, grad_rows), padding)
        grad_probs = cross_cols(grad_rows, values_in[:last_row])
        grad_scores = (probs * (grad_probs - delta[first_row:last_row]) * score_scale).astype(
            jnp.bfloat16
        )
        query_parts.append(
            jnp.dot(grad_scores, keys_in[:last_row], preferred_element_type=jnp.float32)
        )
        grad_keys = grad_keys + jnp.pad(
            cross_rows(grad_scores, queries[first_row:last_row]), padding
        )
    return (jnp.concatenate(query_parts, axis=0), grad_keys, grad_values)


MESH = pl.DeviceIdType.MESH


def vector_sums(fsdp, tp, all_rows, rows_ref, out_ref, first, second, send, recv, send2, recv2):
    f = lax.axis_index("fsdp")
    t = lax.axis_index("tp")
    barrier = pltpu.get_barrier_semaphore()

    def greet_f(step, carry):
        pl.semaphore_signal(
            barrier, inc=1, device_id=(lax.rem(f + step, fsdp), t), device_id_type=MESH
        )
        return carry

    def greet_t(step, carry):
        pl.semaphore_signal(
            barrier, inc=1, device_id=(f, lax.rem(t + step, tp)), device_id_type=MESH
        )
        return carry

    lax.fori_loop(1, fsdp, greet_f, 0)
    lax.fori_loop(1, tp, greet_t, 0)
    pl.semaphore_wait(barrier, fsdp + tp - 2)

    def copy_f(step, source):
        return pltpu.make_async_remote_copy(
            src_ref=rows_ref,
            dst_ref=first.at[source],
            send_sem=send.at[step],
            recv_sem=recv.at[step],
            device_id=(lax.rem(f + step, fsdp), t),
            device_id_type=MESH,
        )

    def start_f(step, carry):
        copy_f(step, f).start()
        return carry

    def wait_f(step, carry):
        copy_f(step, lax.rem(f + fsdp - step, fsdp)).wait()
        return carry

    lax.fori_loop(1, fsdp, start_f, 0)
    first[f] = rows_ref[...]
    lax.fori_loop(1, fsdp, wait_f, 0)
    total = lax.fori_loop(
        1, fsdp, lambda step, value: value + first[step], first[0]
    )
    second[t] = total[:all_rows]

    def copy_t(step, source):
        return pltpu.make_async_remote_copy(
            src_ref=second.at[t],
            dst_ref=second.at[source],
            send_sem=send2.at[step],
            recv_sem=recv2.at[step],
            device_id=(f, lax.rem(t + step, tp)),
            device_id_type=MESH,
        )

    for step in range(1, tp):
        copy_t(step, t).start()
    for step in range(1, tp):
        copy_t(step, lax.rem(t + tp - step, tp)).wait()
    whole = second[0]
    for step in range(1, tp):
        whole = whole + second[step]
    out_ref[:all_rows] = whole
    out_ref[all_rows:] = total[all_rows:]


def sum_vectors(rows, all_rows):
    fsdp = lax.axis_size("fsdp")
    tp = lax.axis_size("tp")
    return pl.pallas_call(
        functools.partial(vector_sums, fsdp, tp, all_rows),
        out_shape=jax.ShapeDtypeStruct(rows.shape, jnp.float32),
        in_specs=[pl.BlockSpec(memory_space=pltpu.VMEM)],
        out_specs=pl.BlockSpec(memory_space=pltpu.VMEM),
        scratch_shapes=[
            pltpu.VMEM((fsdp,) + rows.shape, jnp.float32),
            pltpu.VMEM((tp, all_rows, rows.shape[1]), jnp.float32),
            pltpu.SemaphoreType.DMA((fsdp,)),
            pltpu.SemaphoreType.DMA((fsdp,)),
            pltpu.SemaphoreType.DMA((tp,)),
            pltpu.SemaphoreType.DMA((tp,)),
        ],
        compiler_params=pltpu.CompilerParams(collective_id=1, has_side_effects=True),
        name="vector_sums",
    )(rows)


def gather_weights(shard):
    return lax.all_gather(shard, "fsdp", axis=0, tiled=True)


def scatter_grads(grads):
    return lax.psum_scatter(
        grads.astype(jnp.bfloat16), "fsdp", scatter_dimension=0, tiled=True
    )


def scatter_rows(partial):
    return lax.psum_scatter(
        partial.astype(jnp.bfloat16), "tp", scatter_dimension=0, tiled=True
    ).astype(jnp.float32)


def attention_branch(features, grad_rows, qkv_full, qkv_bias, out_full, segment_row):
    score_scale = HEAD_DIM ** (-0.5)
    length = features.shape[0]
    local_heads = qkv_full.shape[1] // (3 * HEAD_DIM)
    cos_table, sin_table = rotary_tables(positions_of(segment_row))
    packed = (jnp.dot(features, qkv_full, preferred_element_type=jnp.float32) + qkv_bias).reshape(
        length, local_heads, 3, HEAD_DIM
    )
    queries = rotate(packed[:, :, 0], cos_table, sin_table).astype(jnp.bfloat16).transpose(1, 0, 2)
    keys_all = rotate(packed[:, :, 1], cos_table, sin_table).astype(jnp.bfloat16).transpose(1, 0, 2)
    values_all = packed[:, :, 2].astype(jnp.bfloat16).transpose(1, 0, 2)

    def forward_head(member):
        return head_forward(member[0], member[1], member[2], segment_row, score_scale)

    mixed, log_total = lax.map(forward_head, (queries, keys_all, values_all))
    mixed_rows = mixed.transpose(1, 0, 2).reshape(length, local_heads * HEAD_DIM)
    mixed_grad = (
        jnp.dot(grad_rows, out_full, preferred_element_type=jnp.float32)
        .astype(jnp.bfloat16)
        .reshape(length, local_heads, HEAD_DIM)
        .transpose(1, 0, 2)
    )

    def backward_head(member):
        return head_backward(*member, segment_row, score_scale)

    grad_q, grad_k, grad_v = lax.map(
        backward_head, (queries, keys_all, values_all, mixed, mixed_grad, log_total)
    )
    grad_q = unrotate(grad_q.transpose(1, 0, 2), cos_table, sin_table)
    grad_k = unrotate(grad_k.transpose(1, 0, 2), cos_table, sin_table)
    grad_v = grad_v.transpose(1, 0, 2)
    packed_grad = jnp.stack([grad_q, grad_k, grad_v], axis=2).reshape(
        length, 3 * local_heads * HEAD_DIM
    )
    return mixed_rows, packed_grad.astype(jnp.bfloat16), jnp.sum(packed_grad, axis=0)


def body(
    layer_input,
    out_cotangent,
    segments,
    norm_gain,
    norm_bias,
    qkv_weight,
    qkv_bias,
    out_weight,
    out_bias,
    up_weight,
    up_bias,
    down_weight,
    down_bias,
):
    width_qkv = qkv_weight.shape[1]
    width_out = out_weight.shape[0]
    width_up = up_weight.shape[1]
    own_rows = layer_input.astype(jnp.float32)
    normed, inverse, shifted = layer_norm(own_rows, norm_gain, norm_bias)
    features = lax.all_gather(shifted.astype(jnp.bfloat16), "tp", axis=0, tiled=True)
    mlp_full = gather_weights(jnp.concatenate([up_weight, down_weight.T], axis=1))
    grad_rows = lax.all_gather(out_cotangent, "tp", axis=0, tiled=True)
    att_full = gather_weights(jnp.concatenate([qkv_weight, out_weight.T], axis=1))
    full_up, full_down = mlp_full[:, :width_up], mlp_full[:, width_up:]
    full_qkv, full_out = att_full[:, :width_qkv], att_full[:, width_qkv:]

    pre_act = jnp.dot(features, full_up, preferred_element_type=jnp.float32) + up_bias
    gelu_rows = gelu_value(pre_act).astype(jnp.bfloat16)
    grad_pre = jnp.dot(grad_rows, full_down, preferred_element_type=jnp.float32) * gelu_slope(
        pre_act
    )
    pre_grads = grad_pre.astype(jnp.bfloat16)
    up_bias_part = jnp.sum(grad_pre, axis=0)
    mlp_grad = jnp.concatenate(
        [
            cross_rows(features, pre_grads).astype(jnp.bfloat16),
            cross_rows(grad_rows, gelu_rows).astype(jnp.bfloat16),
        ],
        axis=1,
    )
    features_late, grad_late, mlp_grad, pre_grads = lax.optimization_barrier(
        (features, grad_rows, mlp_grad, pre_grads)
    )
    mlp_sum = scatter_grads(mlp_grad)
    mixed_rows, packed_bf, qkv_bias_part = attention_branch(
        features_late, grad_late, full_qkv, qkv_bias, full_out, segments[0]
    )
    partial_value = cross_cols(mixed_rows, full_out) + cross_cols(gelu_rows, full_down)
    branch = scatter_rows(partial_value)
    feature_grad = cross_cols(packed_bf, full_qkv) + cross_cols(pre_grads, full_up)
    row_grad = scatter_rows(feature_grad)
    att_grad = jnp.concatenate(
        [
            cross_rows(features, packed_bf).astype(jnp.bfloat16),
            cross_rows(grad_rows, mixed_rows).astype(jnp.bfloat16),
        ],
        axis=1,
    )
    att_sum = scatter_grads(att_grad)
    layer_output = (own_rows + branch + out_bias + down_bias).astype(jnp.bfloat16)
    cot_rows = out_cotangent.astype(jnp.float32)
    model = own_rows.shape[1]
    biases = jnp.concatenate([qkv_bias_part, up_bias_part])
    bias_rows = -(-biases.shape[0] // model)
    biases = jnp.pad(biases, (0, bias_rows * model - biases.shape[0])).reshape(bias_rows, model)
    pad_rows = jnp.zeros((8 - 3, model), jnp.float32)
    rows = jnp.concatenate(
        [
            jnp.sum(row_grad * normed, axis=0)[None],
            jnp.sum(row_grad, axis=0)[None],
            jnp.sum(cot_rows, axis=0)[None],
            pad_rows,
            biases,
            jnp.zeros((-bias_rows % 8, model), jnp.float32),
        ]
    )
    sums = sum_vectors(rows, 8)
    gain_grad, shift_grad, bias_grad = sums[0], sums[1], sums[2]
    bias_flat = sums[8 : 8 + bias_rows].reshape(-1)
    qkv_bias_grad = bias_flat[:width_qkv]
    up_bias_grad = bias_flat[width_qkv : width_qkv + width_up]
    scaled = row_grad * norm_gain
    input_grad = (
        cot_rows
        + inverse
        * (
            scaled
            - jnp.mean(scaled, axis=-1, keepdims=True)
            - normed * jnp.mean(scaled * normed, axis=-1, keepdims=True)
        )
    ).astype(jnp.bfloat16)
    mlp_sum = mlp_sum.astype(jnp.float32)
    att_sum = att_sum.astype(jnp.float32)
    return (
        layer_output,
        input_grad,
        gain_grad,
        shift_grad,
        att_sum[:, :width_qkv],
        qkv_bias_grad,
        att_sum[:, width_qkv:].T,
        bias_grad,
        mlp_sum[:, :width_up],
        up_bias_grad,
        mlp_sum[:, width_up:].T,
        bias_grad,
    )


def solution(mesh):
    in_specs = (
        P(("fsdp", "tp"), None),
        P(("fsdp", "tp"), None),
        P("fsdp", None),
        P(),
        P(),
        P("fsdp", "tp"),
        P("tp"),
        P("tp", "fsdp"),
        P(),
        P("fsdp", "tp"),
        P("tp"),
        P("tp", "fsdp"),
        P(),
    )
    out_specs = (
        P(("fsdp", "tp"), None),
        P(("fsdp", "tp"), None),
        P(),
        P(),
        P("fsdp", "tp"),
        P("tp"),
        P("tp", "fsdp"),
        P(),
        P("fsdp", "tp"),
        P("tp"),
        P("tp", "fsdp"),
        P(),
    )
    return jax.shard_map(body, mesh=mesh, in_specs=in_specs, out_specs=out_specs, check_vma=False)
```

```python
import functools

import jax
import jax.numpy as jnp
from jax import lax
from jax.experimental import pallas as pl
from jax.experimental.pallas import tpu as pltpu
from jax.sharding import PartitionSpec as P

HEAD_DIM = 64
ROT = 16


EPSILON = 1e-05
ROTARY_BASE = 10000.0


def layer_norm(values, gain, shift):
    center = values - jnp.mean(values, axis=-1, keepdims=True)
    spread = jnp.mean(center * center, axis=-1, keepdims=True)
    inverse = lax.rsqrt(spread + EPSILON)
    normed = center * inverse
    return (normed, inverse, normed * gain + shift)


def gelu_value(pre_act):
    return 0.5 * pre_act * (1.0 + lax.erf(pre_act * 0.7071067811865476))


def gelu_slope(pre_act):
    return (
        0.5 * (1.0 + lax.erf(pre_act * 0.7071067811865476))
        + pre_act * jnp.exp(-0.5 * pre_act * pre_act) * 0.3989422804014327
    )


def positions_of(segment_row):
    length = segment_row.shape[0]
    counter = jnp.arange(length, dtype=jnp.int32)
    is_start = jnp.concatenate(
        [jnp.ones((1,), dtype=jnp.bool_), segment_row[1:] != segment_row[:-1]]
    )
    starts = lax.cummax(jnp.where(is_start, counter, jnp.zeros_like(counter)), axis=0)
    return counter - starts


def rotary_tables(positions):
    halves = ROT // 2
    inverse_freq = ROTARY_BASE ** (-(jnp.arange(halves, dtype=jnp.float32) * 2.0) / ROT)
    angles = positions.astype(jnp.float32)[:, None] * inverse_freq[None, :]
    cos_table = jnp.cos(angles)
    sin_table = jnp.sin(angles)
    return (
        jnp.concatenate([cos_table, cos_table], axis=-1),
        jnp.concatenate([sin_table, sin_table], axis=-1),
    )


def rotate(tensor, cos_table, sin_table):
    halves = ROT // 2
    turned_part = tensor[..., :ROT]
    turned = jnp.concatenate([-turned_part[..., halves:], turned_part[..., :halves]], axis=-1)
    spun = turned_part * cos_table[:, None, :] + turned * sin_table[:, None, :]
    return jnp.concatenate([spun, tensor[..., ROT:]], axis=-1)


def unrotate(grad_in, cos_table, sin_table):
    halves = ROT // 2
    turned_part = grad_in[..., :ROT]
    scaled = turned_part * sin_table[:, None, :]
    back = jnp.concatenate([scaled[..., halves:], -scaled[..., :halves]], axis=-1)
    return jnp.concatenate(
        [turned_part * cos_table[:, None, :] + back, grad_in[..., ROT:]], axis=-1
    )


def cross_rows(left, right):
    return lax.dot_general(
        left, right, (((0,), (0,)), ((), ())), preferred_element_type=jnp.float32
    )


def cross_cols(left, right):
    return lax.dot_general(
        left, right, (((1,), (1,)), ((), ())), preferred_element_type=jnp.float32
    )


def block_scores(queries, keys_in, segment_row, first_row, last_row, score_scale):
    counter = jnp.arange(last_row, dtype=jnp.int32)
    allowed = (segment_row[first_row:last_row, None] == segment_row[None, :last_row]) & (
        counter[first_row:last_row, None] >= counter[None, :last_row]
    )
    scores = cross_cols(queries[first_row:last_row], keys_in[:last_row]) * score_scale
    return jnp.where(allowed, scores, -jnp.inf)


def head_forward(queries, keys_in, values_in, segment_row, score_scale):
    length = queries.shape[0]
    span = min(512, length)
    mixed_parts = []
    total_parts = []
    for first_row in range(0, length, span):
        last_row = min(first_row + span, length)
        scores = block_scores(queries, keys_in, segment_row, first_row, last_row, score_scale)
        highest = jnp.max(scores, axis=-1, keepdims=True)
        log_total = highest + jnp.log(jnp.sum(jnp.exp(scores - highest), axis=-1, keepdims=True))
        weights = jnp.exp(scores - log_total).astype(jnp.bfloat16)
        mixed_parts.append(
            jnp.dot(weights, values_in[:last_row], preferred_element_type=jnp.float32).astype(
                jnp.bfloat16
            )
        )
        total_parts.append(log_total)
    return (jnp.concatenate(mixed_parts, axis=0), jnp.concatenate(total_parts, axis=0))


def head_backward(
    queries, keys_in, values_in, mixed, grad_mixed, log_total, segment_row, score_scale
):
    length = queries.shape[0]
    span = min(512, length)
    delta = jnp.sum(
        grad_mixed.astype(jnp.float32) * mixed.astype(jnp.float32), axis=-1, keepdims=True
    )
    grad_keys = jnp.zeros(keys_in.shape, jnp.float32)
    grad_values = jnp.zeros(values_in.shape, jnp.float32)
    query_parts = []
    for first_row in range(0, length, span):
        last_row = min(first_row + span, length)
        padding = ((0, length - last_row), (0, 0))
        scores = block_scores(queries, keys_in, segment_row, first_row, last_row, score_scale)
        probs = jnp.exp(scores - log_total[first_row:last_row])
        weights = probs.astype(jnp.bfloat16)
        grad_rows = grad_mixed[first_row:last_row]
        grad_values = grad_values + jnp.pad(cross_rows(weights, grad_rows), padding)
        grad_probs = cross_cols(grad_rows, values_in[:last_row])
        grad_scores = (probs * (grad_probs - delta[first_row:last_row]) * score_scale).astype(
            jnp.bfloat16
        )
        query_parts.append(
            jnp.dot(grad_scores, keys_in[:last_row], preferred_element_type=jnp.float32)
        )
        grad_keys = grad_keys + jnp.pad(
            cross_rows(grad_scores, queries[first_row:last_row]), padding
        )
    return (jnp.concatenate(query_parts, axis=0), grad_keys, grad_values)


MESH = pl.DeviceIdType.MESH


def place(fsdp, tp):
    f = lax.axis_index("fsdp")
    t = lax.axis_index("tp")
    pair = lax.rem(f, 2)
    line = lax.div(f, 2)
    return f, t, pair, line


def remote(source, target, send, recv, device):
    return pltpu.make_async_remote_copy(
        src_ref=source,
        dst_ref=target,
        send_sem=send,
        recv_sem=recv,
        device_id=device,
        device_id_type=MESH,
    )


def each(first, last, action):
    def step_of(step, carry):
        action(step)
        return carry

    lax.fori_loop(first, last, step_of, 0)


def greet(fsdp, tp):
    f, t, _, _ = place(fsdp, tp)
    barrier = pltpu.get_barrier_semaphore()
    each(
        1,
        fsdp,
        lambda step: pl.semaphore_signal(
            barrier, inc=1, device_id=(lax.rem(f + step, fsdp), t), device_id_type=MESH
        ),
    )
    each(
        1,
        tp,
        lambda step: pl.semaphore_signal(
            barrier, inc=1, device_id=(f, lax.rem(t + step, tp)), device_id_type=MESH
        ),
    )
    pl.semaphore_wait(barrier, fsdp + tp - 2)


def gather_kernel(
    fsdp, tp, w_ref, h_ref, c_ref, w_out, h_out, c_out, w_send, w_recv, p_send, p_recv, r_send, r_recv
):
    f, t, pair, line = place(fsdp, tp)
    lines = fsdp // 2
    greet(fsdp, tp)
    partner = 2 * line + 1 - pair

    def along(step, slot):
        other = lax.rem(line + step, lines)
        return remote(
            w_ref, w_out.at[slot], w_send.at[step], w_recv.at[step], (2 * other + pair, t)
        )

    def across(step, source, slot):
        return remote(source, w_out.at[slot], p_send.at[step], p_recv.at[step], (partner, t))

    def beside(step, which, source, target, slot):
        return remote(
            source,
            target.at[slot],
            r_send.at[which, step],
            r_recv.at[which, step],
            (f, lax.rem(t + step, tp)),
        )

    def came(step, side):
        return 2 * lax.rem(line + lines - step, lines) + side

    across(0, w_ref, f).start()
    each(1, lines, lambda step: along(step, f).start())
    each(1, tp, lambda step: beside(step, 0, h_ref, h_out, t).start())
    each(1, tp, lambda step: beside(step, 1, c_ref, c_out, t).start())
    w_out[f] = w_ref[...]
    h_out[t] = h_ref[...]
    c_out[t] = c_ref[...]

    def forward(step):
        slot = came(step, pair)
        along(step, slot).wait_recv()
        across(step, w_out.at[slot], slot).start()

    each(1, lines, forward)

    def settle(step):
        slot = lax.rem(t + tp - step, tp)
        beside(step, 0, h_ref, h_out, slot).wait()
        beside(step, 1, c_ref, c_out, slot).wait()

    each(1, tp, settle)
    each(1, lines, lambda step: along(step, f).wait_send())

    def finish(step):
        across(step, w_ref, came(step, 1 - pair)).wait()

    each(0, lines, finish)


def gather_all(weights, features, cotangent):
    fsdp = lax.axis_size("fsdp")
    tp = lax.axis_size("tp")
    vmem = pl.BlockSpec(memory_space=pltpu.VMEM)
    shapes = (
        jax.ShapeDtypeStruct((fsdp,) + weights.shape, weights.dtype),
        jax.ShapeDtypeStruct((tp,) + features.shape, features.dtype),
        jax.ShapeDtypeStruct((tp,) + cotangent.shape, cotangent.dtype),
    )
    dma = pltpu.SemaphoreType.DMA
    w_all, h_all, c_all = pl.pallas_call(
        functools.partial(gather_kernel, fsdp, tp),
        out_shape=shapes,
        in_specs=[vmem] * 3,
        out_specs=(vmem,) * 3,
        scratch_shapes=[
            dma((fsdp // 2,)),
            dma((fsdp // 2,)),
            dma((fsdp // 2,)),
            dma((fsdp // 2,)),
            dma((2, tp)),
            dma((2, tp)),
        ],
        compiler_params=pltpu.CompilerParams(
            collective_id=1, has_side_effects=True, vmem_limit_bytes=48 * 1024 * 1024
        ),
        name="gather_all",
    )(weights, features, cotangent)
    return (
        w_all.reshape(fsdp * weights.shape[0], weights.shape[1]),
        h_all.reshape(tp * features.shape[0], features.shape[1]),
        c_all.reshape(tp * cotangent.shape[0], cotangent.shape[1]),
    )


def scatter_kernel(
    fsdp,
    tp,
    g_ref,
    b_ref,
    d_ref,
    n_ref,
    v_ref,
    g_out,
    b_out,
    d_out,
    v_out,
    halves,
    joined,
    lands,
    b_land,
    d_land,
    rows,
    first,
    second,
    p_send,
    p_recv,
    w_send,
    w_recv,
    r_send,
    r_recv,
    v_send,
    v_recv,
    u_send,
    u_recv,
):
    f, t, pair, line = place(fsdp, tp)
    lines = fsdp // 2
    greet(fsdp, tp)
    partner = 2 * line + 1 - pair

    def ahead(step):
        return lax.rem(line + step, lines)

    def across(step):
        return remote(
            g_ref.at[2 * ahead(step) + 1 - pair],
            halves.at[step],
            p_send.at[step],
            p_recv.at[step],
            (partner, t),
        )

    def along(step):
        return remote(
            joined.at[step],
            lands.at[step],
            w_send.at[step],
            w_recv.at[step],
            (2 * ahead(step) + pair, t),
        )

    def beside(step, which, source, target):
        return remote(
            source.at[lax.rem(t + step, tp)],
            target.at[step],
            r_send.at[which, step],
            r_recv.at[which, step],
            (f, lax.rem(t + step, tp)),
        )

    def start_beside(step):
        beside(step, 1, d_ref, d_land).start()
        beside(step, 0, b_ref, b_land).start()

    each(1, lines, lambda step: across(step).start())
    across(0).start()
    each(1, tp, start_beside)

    def join(step):
        across(step).wait_recv()
        joined[step] = (
            g_ref[2 * ahead(step) + pair].astype(jnp.float32)
            + halves[step].astype(jnp.float32)
        ).astype(joined.dtype)
        along(step).start()

    each(1, lines, join)
    across(0).wait_recv()
    g_out[...] = g_ref[f].astype(jnp.float32) + halves[0].astype(jnp.float32)

    d_out[...] = d_ref[t].astype(jnp.float32)
    b_out[...] = b_ref[t].astype(jnp.float32)

    def gather_d(step):
        beside(step, 1, d_ref, d_land).wait()
        d_out[...] += d_land[step].astype(jnp.float32)

    def gather_b(step):
        beside(step, 0, b_ref, b_land).wait()
        b_out[...] += b_land[step].astype(jnp.float32)

    each(1, tp, gather_d)
    rows[...] = v_ref[...]
    rows[0:1] = jnp.sum(d_out[...] * n_ref[...], axis=0, keepdims=True)
    rows[1:2] = jnp.sum(d_out[...], axis=0, keepdims=True)

    def spread(step, slot):
        return remote(
            rows,
            first.at[slot],
            v_send.at[step],
            v_recv.at[step],
            (lax.rem(f + step, fsdp), t),
        )

    each(1, fsdp, lambda step: spread(step, f).start())
    first[f] = rows[...]
    each(1, tp, gather_b)

    def collect(step):
        along(step).wait_recv()
        g_out[...] += lands[step].astype(jnp.float32)

    each(1, lines, collect)
    each(1, fsdp, lambda step: spread(step, lax.rem(f + fsdp - step, fsdp)).wait())
    total = lax.fori_loop(1, fsdp, lambda step, value: value + first[step], first[0])
    second[t] = total[:8]
    v_out[...] = total

    def share(step, slot):
        return remote(
            second.at[t],
            second.at[slot],
            u_send.at[step],
            u_recv.at[step],
            (f, lax.rem(t + step, tp)),
        )

    each(1, tp, lambda step: share(step, t).start())
    each(1, lines, lambda step: along(step).wait_send())
    each(0, lines, lambda step: across(step).wait_send())
    each(1, tp, lambda step: share(step, lax.rem(t + tp - step, tp)).wait())
    whole = second[0]
    for step in range(1, tp):
        whole = whole + second[step]
    v_out[:8] = whole


def scatter_all(grads, branch, feature_grad, normed, vectors):
    fsdp = lax.axis_size("fsdp")
    tp = lax.axis_size("tp")
    lines = fsdp // 2
    grads = grads.reshape(fsdp, -1, grads.shape[1])
    branch = branch.reshape(tp, -1, branch.shape[1])
    feature_grad = feature_grad.reshape(tp, -1, feature_grad.shape[1])
    vmem = pl.BlockSpec(memory_space=pltpu.VMEM)
    dma = pltpu.SemaphoreType.DMA
    f32 = jnp.float32
    return pl.pallas_call(
        functools.partial(scatter_kernel, fsdp, tp),
        out_shape=(
            jax.ShapeDtypeStruct(grads.shape[1:], f32),
            jax.ShapeDtypeStruct(branch.shape[1:], f32),
            jax.ShapeDtypeStruct(feature_grad.shape[1:], f32),
            jax.ShapeDtypeStruct(vectors.shape, f32),
        ),
        in_specs=[vmem] * 5,
        out_specs=(vmem,) * 4,
        scratch_shapes=[
            pltpu.VMEM((lines,) + grads.shape[1:], grads.dtype),
            pltpu.VMEM((lines,) + grads.shape[1:], grads.dtype),
            pltpu.VMEM((lines,) + grads.shape[1:], grads.dtype),
            pltpu.VMEM(branch.shape, branch.dtype),
            pltpu.VMEM(feature_grad.shape, feature_grad.dtype),
            pltpu.VMEM(vectors.shape, f32),
            pltpu.VMEM((fsdp,) + vectors.shape, f32),
            pltpu.VMEM((tp, 8, vectors.shape[1]), f32),
            dma((lines,)),
            dma((lines,)),
            dma((lines,)),
            dma((lines,)),
            dma((2, tp)),
            dma((2, tp)),
            dma((fsdp,)),
            dma((fsdp,)),
            dma((tp,)),
            dma((tp,)),
        ],
        compiler_params=pltpu.CompilerParams(
            collective_id=2, has_side_effects=True, vmem_limit_bytes=56 * 1024 * 1024
        ),
        name="scatter_all",
    )(grads, branch, feature_grad, normed, vectors)


def attention_branch(features, grad_rows, qkv_full, qkv_bias, out_full, segment_row):
    score_scale = HEAD_DIM ** (-0.5)
    length = features.shape[0]
    local_heads = qkv_full.shape[1] // (3 * HEAD_DIM)
    cos_table, sin_table = rotary_tables(positions_of(segment_row))
    packed = (jnp.dot(features, qkv_full, preferred_element_type=jnp.float32) + qkv_bias).reshape(
        length, local_heads, 3, HEAD_DIM
    )
    queries = rotate(packed[:, :, 0], cos_table, sin_table).astype(jnp.bfloat16).transpose(1, 0, 2)
    keys_all = rotate(packed[:, :, 1], cos_table, sin_table).astype(jnp.bfloat16).transpose(1, 0, 2)
    values_all = packed[:, :, 2].astype(jnp.bfloat16).transpose(1, 0, 2)

    def forward_head(member):
        return head_forward(member[0], member[1], member[2], segment_row, score_scale)

    mixed, log_total = lax.map(forward_head, (queries, keys_all, values_all))
    mixed_rows = mixed.transpose(1, 0, 2).reshape(length, local_heads * HEAD_DIM)
    mixed_grad = (
        jnp.dot(grad_rows, out_full, preferred_element_type=jnp.float32)
        .astype(jnp.bfloat16)
        .reshape(length, local_heads, HEAD_DIM)
        .transpose(1, 0, 2)
    )

    def backward_head(member):
        return head_backward(*member, segment_row, score_scale)

    grad_q, grad_k, grad_v = lax.map(
        backward_head, (queries, keys_all, values_all, mixed, mixed_grad, log_total)
    )
    grad_q = unrotate(grad_q.transpose(1, 0, 2), cos_table, sin_table)
    grad_k = unrotate(grad_k.transpose(1, 0, 2), cos_table, sin_table)
    grad_v = grad_v.transpose(1, 0, 2)
    packed_grad = jnp.stack([grad_q, grad_k, grad_v], axis=2).reshape(
        length, 3 * local_heads * HEAD_DIM
    )
    return mixed_rows, packed_grad.astype(jnp.bfloat16), jnp.sum(packed_grad, axis=0)


def body(
    layer_input,
    out_cotangent,
    segments,
    norm_gain,
    norm_bias,
    qkv_weight,
    qkv_bias,
    out_weight,
    out_bias,
    up_weight,
    up_bias,
    down_weight,
    down_bias,
):
    width_qkv = qkv_weight.shape[1]
    width_out = out_weight.shape[0]
    width_up = up_weight.shape[1]
    own_rows = layer_input.astype(jnp.float32)
    normed, inverse, shifted = layer_norm(own_rows, norm_gain, norm_bias)
    w_all, features, grad_rows = gather_all(
        jnp.concatenate([up_weight, down_weight.T, qkv_weight, out_weight.T], axis=1),
        shifted.astype(jnp.bfloat16),
        out_cotangent,
    )
    ends = (width_up, 2 * width_up, 2 * width_up + width_qkv)
    full_up, full_down, full_qkv, full_out = jnp.split(w_all, ends, axis=1)

    pre_act = jnp.dot(features, full_up, preferred_element_type=jnp.float32) + up_bias
    gelu_rows = gelu_value(pre_act).astype(jnp.bfloat16)
    grad_pre = jnp.dot(grad_rows, full_down, preferred_element_type=jnp.float32) * gelu_slope(
        pre_act
    )
    pre_grads = grad_pre.astype(jnp.bfloat16)
    up_bias_part = jnp.sum(grad_pre, axis=0)
    mixed_rows, packed_bf, qkv_bias_part = attention_branch(
        features, grad_rows, full_qkv, qkv_bias, full_out, segments[0]
    )
    branch = cross_cols(mixed_rows, full_out) + cross_cols(gelu_rows, full_down)
    feature_grad = cross_cols(packed_bf, full_qkv) + cross_cols(pre_grads, full_up)
    grads = jnp.concatenate(
        [
            cross_rows(features, pre_grads).astype(jnp.bfloat16),
            cross_rows(grad_rows, gelu_rows).astype(jnp.bfloat16),
            cross_rows(features, packed_bf).astype(jnp.bfloat16),
            cross_rows(grad_rows, mixed_rows).astype(jnp.bfloat16),
        ],
        axis=1,
    )
    cot_rows = out_cotangent.astype(jnp.float32)
    model = own_rows.shape[1]
    biases = jnp.concatenate([qkv_bias_part, up_bias_part])
    bias_rows = -(-biases.shape[0] // model)
    biases = jnp.pad(biases, (0, bias_rows * model - biases.shape[0])).reshape(bias_rows, model)
    vectors = jnp.concatenate(
        [
            jnp.zeros((2, model), jnp.float32),
            jnp.sum(cot_rows, axis=0)[None],
            jnp.zeros((5, model), jnp.float32),
            biases,
            jnp.zeros((-bias_rows % 8, model), jnp.float32),
        ]
    )
    grad_sum, branch, row_grad, sums = scatter_all(
        grads,
        branch.astype(jnp.bfloat16),
        feature_grad.astype(jnp.bfloat16),
        normed,
        vectors,
    )
    layer_output = (own_rows + branch + out_bias + down_bias).astype(jnp.bfloat16)
    gain_grad, shift_grad, bias_grad = sums[0], sums[1], sums[2]
    bias_flat = sums[8 : 8 + bias_rows].reshape(-1)
    qkv_bias_grad = bias_flat[:width_qkv]
    up_bias_grad = bias_flat[width_qkv : width_qkv + width_up]
    scaled = row_grad * norm_gain
    input_grad = (
        cot_rows
        + inverse
        * (
            scaled
            - jnp.mean(scaled, axis=-1, keepdims=True)
            - normed * jnp.mean(scaled * normed, axis=-1, keepdims=True)
        )
    ).astype(jnp.bfloat16)
    up_grad, down_grad, qkv_grad, out_grad = jnp.split(grad_sum, ends, axis=1)
    return (
        layer_output,
        input_grad,
        gain_grad,
        shift_grad,
        qkv_grad,
        qkv_bias_grad,
        out_grad.T,
        bias_grad,
        up_grad,
        up_bias_grad,
        down_grad.T,
        bias_grad,
    )


def solution(mesh):
    in_specs = (
        P(("fsdp", "tp"), None),
        P(("fsdp", "tp"), None),
        P("fsdp", None),
        P(),
        P(),
        P("fsdp", "tp"),
        P("tp"),
        P("tp", "fsdp"),
        P(),
        P("fsdp", "tp"),
        P("tp"),
        P("tp", "fsdp"),
        P(),
    )
    out_specs = (
        P(("fsdp", "tp"), None),
        P(("fsdp", "tp"), None),
        P(),
        P(),
        P("fsdp", "tp"),
        P("tp"),
        P("tp", "fsdp"),
        P(),
        P("fsdp", "tp"),
        P("tp"),
        P("tp", "fsdp"),
        P(),
    )
    return jax.shard_map(body, mesh=mesh, in_specs=in_specs, out_specs=out_specs, check_vma=False)
```

```python
import functools

import jax
import jax.numpy as jnp
from jax import lax
from jax.experimental import pallas as pl
from jax.experimental.pallas import tpu as pltpu
from jax.sharding import PartitionSpec as P

HEAD_DIM = 64
ROT = 16


EPSILON = 1e-05
ROTARY_BASE = 10000.0


def layer_norm(values, gain, shift):
    center = values - jnp.mean(values, axis=-1, keepdims=True)
    spread = jnp.mean(center * center, axis=-1, keepdims=True)
    inverse = lax.rsqrt(spread + EPSILON)
    normed = center * inverse
    return (normed, inverse, normed * gain + shift)


def gelu_value(pre_act):
    return 0.5 * pre_act * (1.0 + lax.erf(pre_act * 0.7071067811865476))


def gelu_slope(pre_act):
    return (
        0.5 * (1.0 + lax.erf(pre_act * 0.7071067811865476))
        + pre_act * jnp.exp(-0.5 * pre_act * pre_act) * 0.3989422804014327
    )


def positions_of(segment_row):
    length = segment_row.shape[0]
    counter = jnp.arange(length, dtype=jnp.int32)
    is_start = jnp.concatenate(
        [jnp.ones((1,), dtype=jnp.bool_), segment_row[1:] != segment_row[:-1]]
    )
    starts = lax.cummax(jnp.where(is_start, counter, jnp.zeros_like(counter)), axis=0)
    return counter - starts


def rotary_tables(positions):
    halves = ROT // 2
    inverse_freq = ROTARY_BASE ** (-(jnp.arange(halves, dtype=jnp.float32) * 2.0) / ROT)
    angles = positions.astype(jnp.float32)[:, None] * inverse_freq[None, :]
    cos_table = jnp.cos(angles)
    sin_table = jnp.sin(angles)
    return (
        jnp.concatenate([cos_table, cos_table], axis=-1),
        jnp.concatenate([sin_table, sin_table], axis=-1),
    )


def cross_rows(left, right):
    return lax.dot_general(
        left, right, (((0,), (0,)), ((), ())), preferred_element_type=jnp.float32
    )


def cross_cols(left, right):
    return lax.dot_general(
        left, right, (((1,), (1,)), ((), ())), preferred_element_type=jnp.float32
    )


MESH = pl.DeviceIdType.MESH


def place(fsdp, tp):
    f = lax.axis_index("fsdp")
    t = lax.axis_index("tp")
    pair = lax.rem(f, 2)
    line = lax.div(f, 2)
    return f, t, pair, line


def remote(source, target, send, recv, device):
    return pltpu.make_async_remote_copy(
        src_ref=source,
        dst_ref=target,
        send_sem=send,
        recv_sem=recv,
        device_id=device,
        device_id_type=MESH,
    )


def each(first, last, action):
    def step_of(step, carry):
        action(step)
        return carry

    lax.fori_loop(first, last, step_of, 0)


def greet(fsdp, tp):
    f, t, _, _ = place(fsdp, tp)
    barrier = pltpu.get_barrier_semaphore()
    each(
        1,
        fsdp,
        lambda step: pl.semaphore_signal(
            barrier, inc=1, device_id=(lax.rem(f + step, fsdp), t), device_id_type=MESH
        ),
    )
    each(
        1,
        tp,
        lambda step: pl.semaphore_signal(
            barrier, inc=1, device_id=(f, lax.rem(t + step, tp)), device_id_type=MESH
        ),
    )
    pl.semaphore_wait(barrier, fsdp + tp - 2)


def gather_kernel(
    fsdp, tp, w_ref, h_ref, c_ref, w_out, h_out, c_out, w_send, w_recv, p_send, p_recv, r_send, r_recv
):
    f, t, pair, line = place(fsdp, tp)
    lines = fsdp // 2
    greet(fsdp, tp)
    partner = 2 * line + 1 - pair

    def along(step, slot):
        other = lax.rem(line + step, lines)
        return remote(
            w_ref, w_out.at[slot], w_send.at[step], w_recv.at[step], (2 * other + pair, t)
        )

    def across(step, source, slot):
        return remote(source, w_out.at[slot], p_send.at[step], p_recv.at[step], (partner, t))

    def beside(step, which, source, target, slot):
        return remote(
            source,
            target.at[slot],
            r_send.at[which, step],
            r_recv.at[which, step],
            (f, lax.rem(t + step, tp)),
        )

    def came(step, side):
        return 2 * lax.rem(line + lines - step, lines) + side

    across(0, w_ref, f).start()
    each(1, lines, lambda step: along(step, f).start())
    each(1, tp, lambda step: beside(step, 0, h_ref, h_out, t).start())
    each(1, tp, lambda step: beside(step, 1, c_ref, c_out, t).start())
    w_out[f] = w_ref[...]
    h_out[t] = h_ref[...]
    c_out[t] = c_ref[...]

    def forward(step):
        slot = came(step, pair)
        along(step, slot).wait_recv()
        across(step, w_out.at[slot], slot).start()

    each(1, lines, forward)

    def settle(step):
        slot = lax.rem(t + tp - step, tp)
        beside(step, 0, h_ref, h_out, slot).wait()
        beside(step, 1, c_ref, c_out, slot).wait()

    each(1, tp, settle)
    each(1, lines, lambda step: along(step, f).wait_send())

    def finish(step):
        across(step, w_ref, came(step, 1 - pair)).wait()

    each(0, lines, finish)


def gather_all(weights, features, cotangent):
    fsdp = lax.axis_size("fsdp")
    tp = lax.axis_size("tp")
    vmem = pl.BlockSpec(memory_space=pltpu.VMEM)
    shapes = (
        jax.ShapeDtypeStruct((fsdp,) + weights.shape, weights.dtype),
        jax.ShapeDtypeStruct((tp,) + features.shape, features.dtype),
        jax.ShapeDtypeStruct((tp,) + cotangent.shape, cotangent.dtype),
    )
    dma = pltpu.SemaphoreType.DMA
    w_all, h_all, c_all = pl.pallas_call(
        functools.partial(gather_kernel, fsdp, tp),
        out_shape=shapes,
        in_specs=[vmem] * 3,
        out_specs=(vmem,) * 3,
        scratch_shapes=[
            dma((fsdp // 2,)),
            dma((fsdp // 2,)),
            dma((fsdp // 2,)),
            dma((fsdp // 2,)),
            dma((2, tp)),
            dma((2, tp)),
        ],
        compiler_params=pltpu.CompilerParams(
            collective_id=1, has_side_effects=True, vmem_limit_bytes=48 * 1024 * 1024
        ),
        name="gather_all",
    )(weights, features, cotangent)
    return (
        w_all.reshape(fsdp * weights.shape[0], weights.shape[1]),
        h_all.reshape(tp * features.shape[0], features.shape[1]),
        c_all.reshape(tp * cotangent.shape[0], cotangent.shape[1]),
    )


def scatter_kernel(
    fsdp,
    tp,
    many,
    *refs,
):
    g_refs, refs = refs[:many], refs[many:]
    b_ref, d_ref, n_ref, v_ref = refs[:4]
    g_outs, refs = refs[4 : 4 + many], refs[4 + many :]
    b_out, d_out, v_out = refs[:3]
    halves, joined, lands = (refs[3 + many * i : 3 + many * (i + 1)] for i in range(3))
    (
        b_land,
        d_land,
        rows,
        first,
        second,
        p_send,
        p_recv,
        w_send,
        w_recv,
        r_send,
        r_recv,
        v_send,
        v_recv,
        u_send,
        u_recv,
    ) = refs[3 + 3 * many :]
    f, t, pair, line = place(fsdp, tp)
    lines = fsdp // 2
    greet(fsdp, tp)
    partner = 2 * line + 1 - pair

    def ahead(step):
        return lax.rem(line + step, lines)

    def across(i, step):
        return remote(
            g_refs[i].at[2 * ahead(step) + 1 - pair],
            halves[i].at[step],
            p_send.at[i, step],
            p_recv.at[i, step],
            (partner, t),
        )

    def along(i, step):
        return remote(
            joined[i].at[step],
            lands[i].at[step],
            w_send.at[i, step],
            w_recv.at[i, step],
            (2 * ahead(step) + pair, t),
        )

    def beside(step, which, source, target):
        return remote(
            source.at[lax.rem(t + step, tp)],
            target.at[step],
            r_send.at[which, step],
            r_recv.at[which, step],
            (f, lax.rem(t + step, tp)),
        )

    def start_beside(step):
        beside(step, 1, d_ref, d_land).start()
        beside(step, 0, b_ref, b_land).start()

    def start_across(step):
        for i in range(many):
            across(i, step).start()

    each(1, lines, start_across)
    start_across(0)
    each(1, tp, start_beside)

    def join(step):
        for i in range(many):
            across(i, step).wait_recv()
            joined[i][step] = (
                g_refs[i][2 * ahead(step) + pair].astype(jnp.float32)
                + halves[i][step].astype(jnp.float32)
            ).astype(joined[i].dtype)
            along(i, step).start()

    each(1, lines, join)
    for i in range(many):
        across(i, 0).wait_recv()
        g_outs[i][...] = g_refs[i][f].astype(jnp.float32) + halves[i][0].astype(jnp.float32)

    d_out[...] = d_ref[t].astype(jnp.float32)
    b_out[...] = b_ref[t].astype(jnp.float32)

    def gather_d(step):
        beside(step, 1, d_ref, d_land).wait()
        d_out[...] += d_land[step].astype(jnp.float32)

    def gather_b(step):
        beside(step, 0, b_ref, b_land).wait()
        b_out[...] += b_land[step].astype(jnp.float32)

    each(1, tp, gather_d)
    rows[...] = v_ref[...]
    rows[0:1] = jnp.sum(d_out[...] * n_ref[...], axis=0, keepdims=True)
    rows[1:2] = jnp.sum(d_out[...], axis=0, keepdims=True)

    def spread(step, slot):
        return remote(
            rows,
            first.at[slot],
            v_send.at[step],
            v_recv.at[step],
            (lax.rem(f + step, fsdp), t),
        )

    each(1, fsdp, lambda step: spread(step, f).start())
    first[f] = rows[...]
    each(1, tp, gather_b)

    def collect(step):
        for i in range(many):
            along(i, step).wait_recv()
            g_outs[i][...] += lands[i][step].astype(jnp.float32)

    each(1, lines, collect)
    each(1, fsdp, lambda step: spread(step, lax.rem(f + fsdp - step, fsdp)).wait())
    total = lax.fori_loop(1, fsdp, lambda step, value: value + first[step], first[0])
    second[t] = total[:8]
    v_out[...] = total

    def share(step, slot):
        return remote(
            second.at[t],
            second.at[slot],
            u_send.at[step],
            u_recv.at[step],
            (f, lax.rem(t + step, tp)),
        )

    each(1, tp, lambda step: share(step, t).start())

    def sent_along(step):
        for i in range(many):
            along(i, step).wait_send()

    def sent_across(step):
        for i in range(many):
            across(i, step).wait_send()

    each(1, lines, sent_along)
    each(0, lines, sent_across)
    each(1, tp, lambda step: share(step, lax.rem(t + tp - step, tp)).wait())
    whole = second[0]
    for step in range(1, tp):
        whole = whole + second[step]
    v_out[:8] = whole


def scatter_all(grads, branch, feature_grad, normed, vectors):
    fsdp = lax.axis_size("fsdp")
    tp = lax.axis_size("tp")
    lines = fsdp // 2
    grads = [grad.reshape(fsdp, -1, grad.shape[1]) for grad in grads]
    many = len(grads)
    branch = branch.reshape(tp, -1, branch.shape[1])
    feature_grad = feature_grad.reshape(tp, -1, feature_grad.shape[1])
    vmem = pl.BlockSpec(memory_space=pltpu.VMEM)
    dma = pltpu.SemaphoreType.DMA
    f32 = jnp.float32
    return pl.pallas_call(
        functools.partial(scatter_kernel, fsdp, tp, many),
        out_shape=(
            *(jax.ShapeDtypeStruct(grad.shape[1:], f32) for grad in grads),
            jax.ShapeDtypeStruct(branch.shape[1:], f32),
            jax.ShapeDtypeStruct(feature_grad.shape[1:], f32),
            jax.ShapeDtypeStruct(vectors.shape, f32),
        ),
        in_specs=[vmem] * (many + 4),
        out_specs=(vmem,) * (many + 3),
        scratch_shapes=[
            *(
                pltpu.VMEM((lines,) + grad.shape[1:], grad.dtype)
                for _ in range(3)
                for grad in grads
            ),
            pltpu.VMEM(branch.shape, branch.dtype),
            pltpu.VMEM(feature_grad.shape, feature_grad.dtype),
            pltpu.VMEM(vectors.shape, f32),
            pltpu.VMEM((fsdp,) + vectors.shape, f32),
            pltpu.VMEM((tp, 8, vectors.shape[1]), f32),
            dma((many, lines)),
            dma((many, lines)),
            dma((many, lines)),
            dma((many, lines)),
            dma((2, tp)),
            dma((2, tp)),
            dma((fsdp,)),
            dma((fsdp,)),
            dma((tp,)),
            dma((tp,)),
        ],
        compiler_params=pltpu.CompilerParams(
            collective_id=2, has_side_effects=True, vmem_limit_bytes=56 * 1024 * 1024
        ),
        name="scatter_all",
    )(*grads, branch, feature_grad, normed, vectors)


MOST = 512
SPAN = 256


def attention_kernel(
    heads,
    x_ref,
    do_ref,
    cos_ref,
    sin_ref,
    turn_ref,
    col_ref,
    row_ref,
    o_ref,
    dx_ref,
    sum_ref,
    queries,
    keys_in,
    values_in,
    grads_in,
    mixed,
    grad_q,
    grad_k,
    grad_v,
):
    length = x_ref.shape[0]
    span = min(SPAN, length)
    scale = HEAD_DIM ** (-0.5)
    two = 2 * HEAD_DIM
    f32 = jnp.float32
    bf16 = jnp.bfloat16

    def turned(value, axis):
        return lax.dot_general(
            value,
            turn_ref[...],
            (((1,), (axis,)), ((), ())),
            precision=lax.Precision.HIGHEST,
            preferred_element_type=f32,
        )

    for n in range(heads):
        base = 3 * HEAD_DIM * n
        for first in range(0, length, span):
            part = slice(first, first + span)
            both = x_ref[part, base : base + two]
            both = both * cos_ref[part] + turned(both, 0) * sin_ref[part]
            queries[n, part] = both[:, :HEAD_DIM].astype(bf16) * bf16(scale)
            keys_in[n, part] = both[:, HEAD_DIM:].astype(bf16)
            values_in[n, part] = x_ref[part, base + two : base + two + HEAD_DIM].astype(bf16)
            grads_in[n, part] = do_ref[part, n * HEAD_DIM : (n + 1) * HEAD_DIM]
    grad_k[...] = jnp.zeros_like(grad_k)
    grad_v[...] = jnp.zeros_like(grad_v)

    def one_head(n, carry):
        for first in range(0, length, span):
            last = first + span
            low = max(0, (first - MOST) // span * span)
            part = slice(first, last)
            window = slice(low, last)
            q = queries[n, part]
            k = keys_in[n, window]
            v = values_in[n, window]
            g = grads_in[n, part]
            shape = (span, last - low)
            allowed = (col_ref[part] == row_ref[:, window]) & (
                lax.broadcasted_iota(jnp.int32, shape, 0) + first
                >= lax.broadcasted_iota(jnp.int32, shape, 1) + low
            )
            scores = jnp.where(allowed, cross_cols(q, k), -1e30)
            exps = jnp.exp(scores - jnp.max(scores, axis=-1, keepdims=True))
            probs = exps * (1.0 / jnp.sum(exps, axis=-1, keepdims=True))
            weights = probs.astype(bf16)
            out = jnp.dot(weights, v, preferred_element_type=f32).astype(bf16)
            mixed[n, part] = out
            delta = jnp.sum(g.astype(f32) * out.astype(f32), axis=-1, keepdims=True)
            grad_probs = cross_cols(g, v)
            grad_scores = (probs * (grad_probs - delta)).astype(bf16)
            grad_q[n, part] = jnp.dot(grad_scores, k, preferred_element_type=f32) * scale
            grad_k[n, window] += cross_rows(grad_scores, q)
            grad_v[n, window] += cross_rows(weights, g)
        return carry

    lax.fori_loop(0, heads, one_head, 0)

    sum_ref[...] = jnp.zeros_like(sum_ref)
    for first in range(0, length, span):
        part = slice(first, first + span)
        pieces = []
        for n in range(heads):
            both = jnp.concatenate([grad_q[n, part], grad_k[n, part]], axis=1)
            both = both * cos_ref[part] + turned(both * sin_ref[part], 1)
            pieces += [both, grad_v[n, part]]
        whole = jnp.concatenate(pieces, axis=1)
        sum_ref[...] += jnp.sum(whole, axis=0, keepdims=True)
        dx_ref[part] = whole.astype(bf16)
        o_ref[part] = jnp.concatenate([mixed[n, part] for n in range(heads)], axis=1)


def attention_branch(features, grad_rows, qkv_full, qkv_bias, out_full, segment_row):
    length = features.shape[0]
    heads = qkv_full.shape[1] // (3 * HEAD_DIM)
    cos_table, sin_table = rotary_tables(positions_of(segment_row))
    rest = ((0, 0), (0, HEAD_DIM - ROT))
    cos_full = jnp.tile(jnp.pad(cos_table, rest, constant_values=1.0), (1, 2))
    sin_full = jnp.tile(jnp.pad(sin_table, rest), (1, 2))
    half = ROT // 2
    source = jnp.arange(2 * HEAD_DIM)[:, None]
    target = jnp.arange(2 * HEAD_DIM)[None, :]
    inner = target % HEAD_DIM
    turn = jnp.where(
        (inner < half) & (source == target + half),
        -1.0,
        jnp.where((inner >= half) & (inner < ROT) & (source == target - half), 1.0, 0.0),
    ).astype(jnp.float32)
    packed = jnp.dot(features, qkv_full, preferred_element_type=jnp.float32) + qkv_bias
    mixed_grad = jnp.dot(grad_rows, out_full, preferred_element_type=jnp.float32).astype(
        jnp.bfloat16
    )
    wide = packed.shape[1]
    vmem = pl.BlockSpec(memory_space=pltpu.VMEM)
    mixed_rows, packed_grad, sums = pl.pallas_call(
        functools.partial(attention_kernel, heads),
        out_shape=(
            jax.ShapeDtypeStruct((length, heads * HEAD_DIM), jnp.bfloat16),
            jax.ShapeDtypeStruct((length, wide), jnp.bfloat16),
            jax.ShapeDtypeStruct((1, wide), jnp.float32),
        ),
        in_specs=[vmem] * 7,
        out_specs=(vmem,) * 3,
        scratch_shapes=[pltpu.VMEM((heads, length, HEAD_DIM), jnp.bfloat16)] * 5
        + [pltpu.VMEM((heads, length, HEAD_DIM), jnp.float32)] * 3,
        compiler_params=pltpu.CompilerParams(vmem_limit_bytes=56 * 1024 * 1024),
        name="attention",
    )(packed, mixed_grad, cos_full, sin_full, turn, segment_row[:, None], segment_row[None, :])
    return mixed_rows, packed_grad, sums[0]


def body(
    layer_input,
    out_cotangent,
    segments,
    norm_gain,
    norm_bias,
    qkv_weight,
    qkv_bias,
    out_weight,
    out_bias,
    up_weight,
    up_bias,
    down_weight,
    down_bias,
):
    width_qkv = qkv_weight.shape[1]
    width_out = out_weight.shape[0]
    width_up = up_weight.shape[1]
    own_rows = layer_input.astype(jnp.float32)
    normed, inverse, shifted = layer_norm(own_rows, norm_gain, norm_bias)
    w_all, features, grad_rows = gather_all(
        jnp.concatenate([up_weight, down_weight.T, qkv_weight, out_weight.T], axis=1),
        shifted.astype(jnp.bfloat16),
        out_cotangent,
    )
    ends = (width_up, 2 * width_up, 2 * width_up + width_qkv)
    full_up, full_down, full_qkv, full_out = jnp.split(w_all, ends, axis=1)

    pre_act = jnp.dot(features, full_up, preferred_element_type=jnp.float32) + up_bias
    gelu_rows = gelu_value(pre_act).astype(jnp.bfloat16)
    grad_pre = jnp.dot(grad_rows, full_down, preferred_element_type=jnp.float32) * gelu_slope(
        pre_act
    )
    pre_grads = grad_pre.astype(jnp.bfloat16)
    up_bias_part = jnp.sum(grad_pre, axis=0)
    mixed_rows, packed_bf, qkv_bias_part = attention_branch(
        features, grad_rows, full_qkv, qkv_bias, full_out, segments[0]
    )
    branch = cross_cols(mixed_rows, full_out) + cross_cols(gelu_rows, full_down)
    feature_grad = cross_cols(packed_bf, full_qkv) + cross_cols(pre_grads, full_up)
    grads = [
        cross_rows(features, pre_grads).astype(jnp.bfloat16),
        cross_rows(grad_rows, gelu_rows).astype(jnp.bfloat16),
        cross_rows(features, packed_bf).astype(jnp.bfloat16),
        cross_rows(grad_rows, mixed_rows).astype(jnp.bfloat16),
    ]
    cot_rows = out_cotangent.astype(jnp.float32)
    model = own_rows.shape[1]
    biases = jnp.concatenate([qkv_bias_part, up_bias_part])
    bias_rows = -(-biases.shape[0] // model)
    biases = jnp.pad(biases, (0, bias_rows * model - biases.shape[0])).reshape(bias_rows, model)
    vectors = jnp.concatenate(
        [
            jnp.zeros((2, model), jnp.float32),
            jnp.sum(cot_rows, axis=0)[None],
            jnp.zeros((5, model), jnp.float32),
            biases,
            jnp.zeros((-bias_rows % 8, model), jnp.float32),
        ]
    )
    up_grad, down_grad, qkv_grad, out_grad, branch, row_grad, sums = scatter_all(
        grads,
        branch.astype(jnp.bfloat16),
        feature_grad.astype(jnp.bfloat16),
        normed,
        vectors,
    )
    layer_output = (own_rows + branch + out_bias + down_bias).astype(jnp.bfloat16)
    gain_grad, shift_grad, bias_grad = sums[0], sums[1], sums[2]
    bias_flat = sums[8 : 8 + bias_rows].reshape(-1)
    qkv_bias_grad = bias_flat[:width_qkv]
    up_bias_grad = bias_flat[width_qkv : width_qkv + width_up]
    scaled = row_grad * norm_gain
    input_grad = (
        cot_rows
        + inverse
        * (
            scaled
            - jnp.mean(scaled, axis=-1, keepdims=True)
            - normed * jnp.mean(scaled * normed, axis=-1, keepdims=True)
        )
    ).astype(jnp.bfloat16)
    return (
        layer_output,
        input_grad,
        gain_grad,
        shift_grad,
        qkv_grad,
        qkv_bias_grad,
        out_grad.T,
        bias_grad,
        up_grad,
        up_bias_grad,
        down_grad.T,
        bias_grad,
    )


def solution(mesh):
    in_specs = (
        P(("fsdp", "tp"), None),
        P(("fsdp", "tp"), None),
        P("fsdp", None),
        P(),
        P(),
        P("fsdp", "tp"),
        P("tp"),
        P("tp", "fsdp"),
        P(),
        P("fsdp", "tp"),
        P("tp"),
        P("tp", "fsdp"),
        P(),
    )
    out_specs = (
        P(("fsdp", "tp"), None),
        P(("fsdp", "tp"), None),
        P(),
        P(),
        P("fsdp", "tp"),
        P("tp"),
        P("tp", "fsdp"),
        P(),
        P("fsdp", "tp"),
        P("tp"),
        P("tp", "fsdp"),
        P(),
    )
    return jax.shard_map(body, mesh=mesh, in_specs=in_specs, out_specs=out_specs, check_vma=False)
```

```python
import functools

import jax
import jax.numpy as jnp
from jax import lax
from jax.experimental import pallas as pl
from jax.experimental.pallas import tpu as pltpu
from jax.sharding import PartitionSpec as P

HEAD_DIM = 64
ROT = 16


EPSILON = 1e-05
ROTARY_BASE = 10000.0


def layer_norm(values, gain, shift):
    center = values - jnp.mean(values, axis=-1, keepdims=True)
    spread = jnp.mean(center * center, axis=-1, keepdims=True)
    inverse = lax.rsqrt(spread + EPSILON)
    normed = center * inverse
    return (normed, inverse, normed * gain + shift)


def gelu_value(pre_act):
    return 0.5 * pre_act * (1.0 + lax.erf(pre_act * 0.7071067811865476))


def gelu_slope(pre_act):
    return (
        0.5 * (1.0 + lax.erf(pre_act * 0.7071067811865476))
        + pre_act * jnp.exp(-0.5 * pre_act * pre_act) * 0.3989422804014327
    )


def positions_of(segment_row):
    length = segment_row.shape[0]
    counter = jnp.arange(length, dtype=jnp.int32)
    is_start = jnp.concatenate(
        [jnp.ones((1,), dtype=jnp.bool_), segment_row[1:] != segment_row[:-1]]
    )
    starts = lax.cummax(jnp.where(is_start, counter, jnp.zeros_like(counter)), axis=0)
    return counter - starts


def rotary_tables(positions):
    halves = ROT // 2
    inverse_freq = ROTARY_BASE ** (-(jnp.arange(halves, dtype=jnp.float32) * 2.0) / ROT)
    angles = positions.astype(jnp.float32)[:, None] * inverse_freq[None, :]
    cos_table = jnp.cos(angles)
    sin_table = jnp.sin(angles)
    return (
        jnp.concatenate([cos_table, cos_table], axis=-1),
        jnp.concatenate([sin_table, sin_table], axis=-1),
    )


def cross_rows(left, right):
    return lax.dot_general(
        left, right, (((0,), (0,)), ((), ())), preferred_element_type=jnp.float32
    )


def cross_cols(left, right):
    return lax.dot_general(
        left, right, (((1,), (1,)), ((), ())), preferred_element_type=jnp.float32
    )


MESH = pl.DeviceIdType.MESH


def place(fsdp, tp):
    f = lax.axis_index("fsdp")
    t = lax.axis_index("tp")
    pair = lax.rem(f, 2)
    line = lax.div(f, 2)
    return f, t, pair, line


def remote(source, target, send, recv, device):
    return pltpu.make_async_remote_copy(
        src_ref=source,
        dst_ref=target,
        send_sem=send,
        recv_sem=recv,
        device_id=device,
        device_id_type=MESH,
    )


def each(first, last, action):
    def step_of(step, carry):
        action(step)
        return carry

    lax.fori_loop(first, last, step_of, 0)


def greet(fsdp, tp):
    f, t, _, _ = place(fsdp, tp)
    barrier = pltpu.get_barrier_semaphore()
    each(
        1,
        fsdp,
        lambda step: pl.semaphore_signal(
            barrier, inc=1, device_id=(lax.rem(f + step, fsdp), t), device_id_type=MESH
        ),
    )
    each(
        1,
        tp,
        lambda step: pl.semaphore_signal(
            barrier, inc=1, device_id=(f, lax.rem(t + step, tp)), device_id_type=MESH
        ),
    )
    pl.semaphore_wait(barrier, fsdp + tp - 2)


def gather_kernel(
    fsdp, tp, w_ref, h_ref, c_ref, w_out, h_out, c_out, w_send, w_recv, p_send, p_recv, r_send, r_recv
):
    f, t, pair, line = place(fsdp, tp)
    lines = fsdp // 2
    greet(fsdp, tp)
    partner = 2 * line + 1 - pair

    def along(step, slot):
        other = lax.rem(line + step, lines)
        return remote(
            w_ref, w_out.at[slot], w_send.at[step], w_recv.at[step], (2 * other + pair, t)
        )

    def across(step, source, slot):
        return remote(source, w_out.at[slot], p_send.at[step], p_recv.at[step], (partner, t))

    def beside(step, which, source, target, slot):
        return remote(
            source,
            target.at[slot],
            r_send.at[which, step],
            r_recv.at[which, step],
            (f, lax.rem(t + step, tp)),
        )

    def came(step, side):
        return 2 * lax.rem(line + lines - step, lines) + side

    across(0, w_ref, f).start()
    each(1, lines, lambda step: along(step, f).start())
    each(1, tp, lambda step: beside(step, 0, h_ref, h_out, t).start())
    each(1, tp, lambda step: beside(step, 1, c_ref, c_out, t).start())
    w_out[f] = w_ref[...]
    h_out[t] = h_ref[...]
    c_out[t] = c_ref[...]

    def forward(step):
        slot = came(step, pair)
        along(step, slot).wait_recv()
        across(step, w_out.at[slot], slot).start()

    each(1, lines, forward)

    def settle(step):
        slot = lax.rem(t + tp - step, tp)
        beside(step, 0, h_ref, h_out, slot).wait()
        beside(step, 1, c_ref, c_out, slot).wait()

    each(1, tp, settle)
    each(1, lines, lambda step: along(step, f).wait_send())

    def finish(step):
        across(step, w_ref, came(step, 1 - pair)).wait()

    each(0, lines, finish)


def gather_all(weights, features, cotangent):
    fsdp = lax.axis_size("fsdp")
    tp = lax.axis_size("tp")
    vmem = pl.BlockSpec(memory_space=pltpu.VMEM)
    shapes = (
        jax.ShapeDtypeStruct((fsdp,) + weights.shape, weights.dtype),
        jax.ShapeDtypeStruct((tp,) + features.shape, features.dtype),
        jax.ShapeDtypeStruct((tp,) + cotangent.shape, cotangent.dtype),
    )
    dma = pltpu.SemaphoreType.DMA
    w_all, h_all, c_all = pl.pallas_call(
        functools.partial(gather_kernel, fsdp, tp),
        out_shape=shapes,
        in_specs=[vmem] * 3,
        out_specs=(vmem,) * 3,
        scratch_shapes=[
            dma((fsdp // 2,)),
            dma((fsdp // 2,)),
            dma((fsdp // 2,)),
            dma((fsdp // 2,)),
            dma((2, tp)),
            dma((2, tp)),
        ],
        compiler_params=pltpu.CompilerParams(
            collective_id=1, has_side_effects=True, vmem_limit_bytes=48 * 1024 * 1024
        ),
        name="gather_all",
    )(weights, features, cotangent)
    return (
        w_all.reshape(fsdp * weights.shape[0], weights.shape[1]),
        h_all.reshape(tp * features.shape[0], features.shape[1]),
        c_all.reshape(tp * cotangent.shape[0], cotangent.shape[1]),
    )


def scatter_kernel(
    fsdp,
    tp,
    many,
    *refs,
):
    g_refs, refs = refs[:many], refs[many:]
    b_ref, d_ref, n_ref, v_ref = refs[:4]
    g_outs, refs = refs[4 : 4 + many], refs[4 + many :]
    b_out, d_out, v_out = refs[:3]
    halves, joined, lands = (refs[3 + many * i : 3 + many * (i + 1)] for i in range(3))
    (
        b_land,
        d_land,
        rows,
        first,
        second,
        p_send,
        p_recv,
        w_send,
        w_recv,
        r_send,
        r_recv,
        v_send,
        v_recv,
        u_send,
        u_recv,
    ) = refs[3 + 3 * many :]
    f, t, pair, line = place(fsdp, tp)
    lines = fsdp // 2
    greet(fsdp, tp)
    partner = 2 * line + 1 - pair

    def ahead(step):
        return lax.rem(line + step, lines)

    def across(i, step):
        return remote(
            g_refs[i].at[2 * ahead(step) + 1 - pair],
            halves[i].at[step],
            p_send.at[i, step],
            p_recv.at[i, step],
            (partner, t),
        )

    def along(i, step):
        return remote(
            joined[i].at[step],
            lands[i].at[step],
            w_send.at[i, step],
            w_recv.at[i, step],
            (2 * ahead(step) + pair, t),
        )

    def beside(step, which, source, target):
        return remote(
            source.at[lax.rem(t + step, tp)],
            target.at[step],
            r_send.at[which, step],
            r_recv.at[which, step],
            (f, lax.rem(t + step, tp)),
        )

    def start_beside(step):
        beside(step, 1, d_ref, d_land).start()
        beside(step, 0, b_ref, b_land).start()

    def start_across(step):
        for i in range(many):
            across(i, step).start()

    each(1, lines, start_across)
    start_across(0)
    each(1, tp, start_beside)

    def join(step):
        for i in range(many):
            across(i, step).wait_recv()
            joined[i][step] = (
                g_refs[i][2 * ahead(step) + pair].astype(jnp.float32)
                + halves[i][step].astype(jnp.float32)
            ).astype(joined[i].dtype)
            along(i, step).start()

    each(1, lines, join)
    for i in range(many):
        across(i, 0).wait_recv()
        g_outs[i][...] = g_refs[i][f].astype(jnp.float32) + halves[i][0].astype(jnp.float32)

    d_out[...] = d_ref[t].astype(jnp.float32)
    b_out[...] = b_ref[t].astype(jnp.float32)

    def gather_d(step):
        beside(step, 1, d_ref, d_land).wait()
        d_out[...] += d_land[step].astype(jnp.float32)

    def gather_b(step):
        beside(step, 0, b_ref, b_land).wait()
        b_out[...] += b_land[step].astype(jnp.float32)

    each(1, tp, gather_d)
    rows[...] = v_ref[...]
    rows[0:1] = jnp.sum(d_out[...] * n_ref[...], axis=0, keepdims=True)
    rows[1:2] = jnp.sum(d_out[...], axis=0, keepdims=True)

    def spread(step, slot):
        return remote(
            rows,
            first.at[slot],
            v_send.at[step],
            v_recv.at[step],
            (lax.rem(f + step, fsdp), t),
        )

    each(1, fsdp, lambda step: spread(step, f).start())
    first[f] = rows[...]
    each(1, tp, gather_b)

    def collect(step):
        for i in range(many):
            along(i, step).wait_recv()
            g_outs[i][...] += lands[i][step].astype(jnp.float32)

    each(1, lines, collect)
    each(1, fsdp, lambda step: spread(step, lax.rem(f + fsdp - step, fsdp)).wait())
    total = lax.fori_loop(1, fsdp, lambda step, value: value + first[step], first[0])
    second[t] = total[:8]
    v_out[...] = total

    def share(step, slot):
        return remote(
            second.at[t],
            second.at[slot],
            u_send.at[step],
            u_recv.at[step],
            (f, lax.rem(t + step, tp)),
        )

    each(1, tp, lambda step: share(step, t).start())

    def sent_along(step):
        for i in range(many):
            along(i, step).wait_send()

    def sent_across(step):
        for i in range(many):
            across(i, step).wait_send()

    each(1, lines, sent_along)
    each(0, lines, sent_across)
    each(1, tp, lambda step: share(step, lax.rem(t + tp - step, tp)).wait())
    whole = second[0]
    for step in range(1, tp):
        whole = whole + second[step]
    v_out[:8] = whole


def scatter_all(grads, branch, feature_grad, normed, vectors):
    fsdp = lax.axis_size("fsdp")
    tp = lax.axis_size("tp")
    lines = fsdp // 2
    grads = [grad.reshape(fsdp, -1, grad.shape[1]) for grad in grads]
    many = len(grads)
    branch = branch.reshape(tp, -1, branch.shape[1])
    feature_grad = feature_grad.reshape(tp, -1, feature_grad.shape[1])
    vmem = pl.BlockSpec(memory_space=pltpu.VMEM)
    dma = pltpu.SemaphoreType.DMA
    f32 = jnp.float32
    return pl.pallas_call(
        functools.partial(scatter_kernel, fsdp, tp, many),
        out_shape=(
            *(jax.ShapeDtypeStruct(grad.shape[1:], f32) for grad in grads),
            jax.ShapeDtypeStruct(branch.shape[1:], f32),
            jax.ShapeDtypeStruct(feature_grad.shape[1:], f32),
            jax.ShapeDtypeStruct(vectors.shape, f32),
        ),
        in_specs=[vmem] * (many + 4),
        out_specs=(vmem,) * (many + 3),
        scratch_shapes=[
            *(
                pltpu.VMEM((lines,) + grad.shape[1:], grad.dtype)
                for _ in range(3)
                for grad in grads
            ),
            pltpu.VMEM(branch.shape, branch.dtype),
            pltpu.VMEM(feature_grad.shape, feature_grad.dtype),
            pltpu.VMEM(vectors.shape, f32),
            pltpu.VMEM((fsdp,) + vectors.shape, f32),
            pltpu.VMEM((tp, 8, vectors.shape[1]), f32),
            dma((many, lines)),
            dma((many, lines)),
            dma((many, lines)),
            dma((many, lines)),
            dma((2, tp)),
            dma((2, tp)),
            dma((fsdp,)),
            dma((fsdp,)),
            dma((tp,)),
            dma((tp,)),
        ],
        compiler_params=pltpu.CompilerParams(
            collective_id=2, has_side_effects=True, vmem_limit_bytes=56 * 1024 * 1024
        ),
        name="scatter_all",
    )(*grads, branch, feature_grad, normed, vectors)


MOST = 512
SPAN = 256


def attention_kernel(
    heads,
    f_ref,
    c_ref,
    wq_ref,
    bq_ref,
    wo_ref,
    cos_ref,
    sin_ref,
    turn_ref,
    col_ref,
    row_ref,
    o_ref,
    dx_ref,
    sum_ref,
    queries,
    keys_in,
    values_in,
    grads_in,
    mixed,
    grad_q,
    grad_k,
    grad_v,
    x_ref,
    do_ref,
):
    length = f_ref.shape[0]
    span = min(SPAN, length)
    scale = HEAD_DIM ** (-0.5)
    two = 2 * HEAD_DIM
    f32 = jnp.float32
    bf16 = jnp.bfloat16

    def turned(value, axis):
        return lax.dot_general(
            value,
            turn_ref[...],
            (((1,), (axis,)), ((), ())),
            precision=lax.Precision.HIGHEST,
            preferred_element_type=f32,
        )

    for first in range(0, length, span):
        part = slice(first, first + span)
        x_ref[part] = (
            jnp.dot(f_ref[part], wq_ref[...], preferred_element_type=f32) + bq_ref[...]
        )
        do_ref[part] = jnp.dot(c_ref[part], wo_ref[...], preferred_element_type=f32).astype(bf16)
    for n in range(heads):
        base = 3 * HEAD_DIM * n
        for first in range(0, length, span):
            part = slice(first, first + span)
            both = x_ref[part, base : base + two]
            both = both * cos_ref[part] + turned(both, 0) * sin_ref[part]
            queries[n, part] = both[:, :HEAD_DIM].astype(bf16) * bf16(scale)
            keys_in[n, part] = both[:, HEAD_DIM:].astype(bf16)
            values_in[n, part] = x_ref[part, base + two : base + two + HEAD_DIM].astype(bf16)
            grads_in[n, part] = do_ref[part, n * HEAD_DIM : (n + 1) * HEAD_DIM]
    grad_k[...] = jnp.zeros_like(grad_k)
    grad_v[...] = jnp.zeros_like(grad_v)

    def one_head(n, carry):
        for first in range(0, length, span):
            last = first + span
            low = max(0, (first - MOST) // span * span)
            part = slice(first, last)
            window = slice(low, last)
            q = queries[n, part]
            k = keys_in[n, window]
            v = values_in[n, window]
            g = grads_in[n, part]
            shape = (span, last - low)
            allowed = (col_ref[part] == row_ref[:, window]) & (
                lax.broadcasted_iota(jnp.int32, shape, 0) + first
                >= lax.broadcasted_iota(jnp.int32, shape, 1) + low
            )
            scores = jnp.where(allowed, cross_cols(q, k), -1e30)
            exps = jnp.exp(scores - jnp.max(scores, axis=-1, keepdims=True))
            probs = exps * (1.0 / jnp.sum(exps, axis=-1, keepdims=True))
            weights = probs.astype(bf16)
            out = jnp.dot(weights, v, preferred_element_type=f32).astype(bf16)
            mixed[n, part] = out
            delta = jnp.sum(g.astype(f32) * out.astype(f32), axis=-1, keepdims=True)
            grad_probs = cross_cols(g, v)
            grad_scores = (probs * (grad_probs - delta)).astype(bf16)
            grad_q[n, part] = jnp.dot(grad_scores, k, preferred_element_type=f32) * scale
            grad_k[n, window] += cross_rows(grad_scores, q)
            grad_v[n, window] += cross_rows(weights, g)
        return carry

    lax.fori_loop(0, heads, one_head, 0)

    sum_ref[...] = jnp.zeros_like(sum_ref)
    for first in range(0, length, span):
        part = slice(first, first + span)
        pieces = []
        for n in range(heads):
            both = jnp.concatenate([grad_q[n, part], grad_k[n, part]], axis=1)
            both = both * cos_ref[part] + turned(both * sin_ref[part], 1)
            pieces += [both, grad_v[n, part]]
        whole = jnp.concatenate(pieces, axis=1)
        sum_ref[...] += jnp.sum(whole, axis=0, keepdims=True)
        dx_ref[part] = whole.astype(bf16)
        o_ref[part] = jnp.concatenate([mixed[n, part] for n in range(heads)], axis=1)


def attention_branch(features, grad_rows, qkv_full, qkv_bias, out_full, segment_row):
    length = features.shape[0]
    heads = qkv_full.shape[1] // (3 * HEAD_DIM)
    cos_table, sin_table = rotary_tables(positions_of(segment_row))
    rest = ((0, 0), (0, HEAD_DIM - ROT))
    cos_full = jnp.tile(jnp.pad(cos_table, rest, constant_values=1.0), (1, 2))
    sin_full = jnp.tile(jnp.pad(sin_table, rest), (1, 2))
    half = ROT // 2
    source = jnp.arange(2 * HEAD_DIM)[:, None]
    target = jnp.arange(2 * HEAD_DIM)[None, :]
    inner = target % HEAD_DIM
    turn = jnp.where(
        (inner < half) & (source == target + half),
        -1.0,
        jnp.where((inner >= half) & (inner < ROT) & (source == target - half), 1.0, 0.0),
    ).astype(jnp.float32)
    wide = qkv_full.shape[1]
    vmem = pl.BlockSpec(memory_space=pltpu.VMEM)
    mixed_rows, packed_grad, sums = pl.pallas_call(
        functools.partial(attention_kernel, heads),
        out_shape=(
            jax.ShapeDtypeStruct((length, heads * HEAD_DIM), jnp.bfloat16),
            jax.ShapeDtypeStruct((length, wide), jnp.bfloat16),
            jax.ShapeDtypeStruct((1, wide), jnp.float32),
        ),
        in_specs=[vmem] * 10,
        out_specs=(vmem,) * 3,
        scratch_shapes=[pltpu.VMEM((heads, length, HEAD_DIM), jnp.bfloat16)] * 5
        + [pltpu.VMEM((heads, length, HEAD_DIM), jnp.float32)] * 3
        + [
            pltpu.VMEM((length, wide), jnp.float32),
            pltpu.VMEM((length, heads * HEAD_DIM), jnp.bfloat16),
        ],
        compiler_params=pltpu.CompilerParams(vmem_limit_bytes=56 * 1024 * 1024),
        name="attention",
    )(
        features,
        grad_rows,
        qkv_full,
        qkv_bias[None],
        out_full,
        cos_full,
        sin_full,
        turn,
        segment_row[:, None],
        segment_row[None, :],
    )
    return mixed_rows, packed_grad, sums[0]


def body(
    layer_input,
    out_cotangent,
    segments,
    norm_gain,
    norm_bias,
    qkv_weight,
    qkv_bias,
    out_weight,
    out_bias,
    up_weight,
    up_bias,
    down_weight,
    down_bias,
):
    width_qkv = qkv_weight.shape[1]
    width_out = out_weight.shape[0]
    width_up = up_weight.shape[1]
    own_rows = layer_input.astype(jnp.float32)
    normed, inverse, shifted = layer_norm(own_rows, norm_gain, norm_bias)
    w_all, features, grad_rows = gather_all(
        jnp.concatenate([up_weight, down_weight.T, qkv_weight, out_weight.T], axis=1),
        shifted.astype(jnp.bfloat16),
        out_cotangent,
    )
    ends = (width_up, 2 * width_up, 2 * width_up + width_qkv)
    full_up, full_down, full_qkv, full_out = jnp.split(w_all, ends, axis=1)

    pre_act = jnp.dot(features, full_up, preferred_element_type=jnp.float32) + up_bias
    gelu_rows = gelu_value(pre_act).astype(jnp.bfloat16)
    grad_pre = jnp.dot(grad_rows, full_down, preferred_element_type=jnp.float32) * gelu_slope(
        pre_act
    )
    pre_grads = grad_pre.astype(jnp.bfloat16)
    up_bias_part = jnp.sum(grad_pre, axis=0)
    mixed_rows, packed_bf, qkv_bias_part = attention_branch(
        features, grad_rows, full_qkv, qkv_bias, full_out, segments[0]
    )
    branch = cross_cols(mixed_rows, full_out) + cross_cols(gelu_rows, full_down)
    feature_grad = cross_cols(packed_bf, full_qkv) + cross_cols(pre_grads, full_up)
    grads = [
        cross_rows(features, pre_grads).astype(jnp.bfloat16),
        cross_rows(grad_rows, gelu_rows).astype(jnp.bfloat16),
        cross_rows(features, packed_bf).astype(jnp.bfloat16),
        cross_rows(grad_rows, mixed_rows).astype(jnp.bfloat16),
    ]
    cot_rows = out_cotangent.astype(jnp.float32)
    model = own_rows.shape[1]
    biases = jnp.concatenate([qkv_bias_part, up_bias_part])
    bias_rows = -(-biases.shape[0] // model)
    biases = jnp.pad(biases, (0, bias_rows * model - biases.shape[0])).reshape(bias_rows, model)
    vectors = jnp.concatenate(
        [
            jnp.zeros((2, model), jnp.float32),
            jnp.sum(cot_rows, axis=0)[None],
            jnp.zeros((5, model), jnp.float32),
            biases,
            jnp.zeros((-bias_rows % 8, model), jnp.float32),
        ]
    )
    up_grad, down_grad, qkv_grad, out_grad, branch, row_grad, sums = scatter_all(
        grads,
        branch.astype(jnp.bfloat16),
        feature_grad.astype(jnp.bfloat16),
        normed,
        vectors,
    )
    layer_output = (own_rows + branch + out_bias + down_bias).astype(jnp.bfloat16)
    gain_grad, shift_grad, bias_grad = sums[0], sums[1], sums[2]
    bias_flat = sums[8 : 8 + bias_rows].reshape(-1)
    qkv_bias_grad = bias_flat[:width_qkv]
    up_bias_grad = bias_flat[width_qkv : width_qkv + width_up]
    scaled = row_grad * norm_gain
    input_grad = (
        cot_rows
        + inverse
        * (
            scaled
            - jnp.mean(scaled, axis=-1, keepdims=True)
            - normed * jnp.mean(scaled * normed, axis=-1, keepdims=True)
        )
    ).astype(jnp.bfloat16)
    return (
        layer_output,
        input_grad,
        gain_grad,
        shift_grad,
        qkv_grad,
        qkv_bias_grad,
        out_grad.T,
        bias_grad,
        up_grad,
        up_bias_grad,
        down_grad.T,
        bias_grad,
    )


def solution(mesh):
    in_specs = (
        P(("fsdp", "tp"), None),
        P(("fsdp", "tp"), None),
        P("fsdp", None),
        P(),
        P(),
        P("fsdp", "tp"),
        P("tp"),
        P("tp", "fsdp"),
        P(),
        P("fsdp", "tp"),
        P("tp"),
        P("tp", "fsdp"),
        P(),
    )
    out_specs = (
        P(("fsdp", "tp"), None),
        P(("fsdp", "tp"), None),
        P(),
        P(),
        P("fsdp", "tp"),
        P("tp"),
        P("tp", "fsdp"),
        P(),
        P("fsdp", "tp"),
        P("tp"),
        P("tp", "fsdp"),
        P(),
    )
    return jax.shard_map(body, mesh=mesh, in_specs=in_specs, out_specs=out_specs, check_vma=False)
```
